32 devices in a mesh: dp: 16 (over z, x, core), seq: 2 (over y).
Axes of the slice: x: 2, y: 2, z: 4, core: 2. Of those that a mesh axis runs over, the one named last changes fastest.
Arguments:
- hidden_in: bfloat16 [4, 16, 512, 768], P(None, 'dp', 'seq'), may hold values from -6 to 6
- segment_ids: int32 [4, 16, 512], P(None, 'dp', 'seq'), may hold values from 0 to 31, as said below
- segment_counts: int32 [4, 16, 32], P(None, 'dp'), may hold values from 1 to 481, as said below
- pooled_grad: float32 [4, 16, 32, 768], P(None, 'dp'), may hold values from -96 to 96
- qkv_weight: bfloat16 [768, 2304], replicated, may hold values from -0.21875 to 0.21875
- query_bias: float32 [768], replicated, may hold values from -3 to 3
- value_bias: float32 [768], replicated, may hold values from -3 to 3
- out_weight: bfloat16 [768, 768], replicated, may hold values from -1.25 to 1.25
- out_bias: float32 [768], replicated, may hold values from -2.5 to 2.5
- norm1_gain: float32 [768], replicated, may hold values from 0.4 to 1.6
- norm1_shift: float32 [768], replicated, may hold values from -2.5 to 2.5
- up_weight: bfloat16 [768, 3072], replicated, may hold values from -0.21875 to 0.21875
- up_bias: float32 [3072], replicated, may hold values from -3 to 3
- down_weight: bfloat16 [3072, 768], replicated, may hold values from -0.15625 to 0.15625
- down_bias: float32 [768], replicated, may hold values from -2.5 to 2.5
- norm2_gain: float32 [768], replicated, may hold values from 0.4 to 1.6
- norm2_shift: float32 [768], replicated, may hold values from -2.5 to 2.5
Outputs:
- pooled: float32 [4, 16, 32, 768], P(None, 'dp')
- grad_input: bfloat16 [4, 16, 512, 768], P(None, 'dp', 'seq')
- grad_qkv_weight: float32 [768, 2304], replicated
- grad_query_bias: float32 [768], replicated
- grad_value_bias: float32 [768], replicated
- grad_out_weight: float32 [768, 768], replicated
- grad_out_bias: float32 [768], replicated
- grad_norm1_gain: float32 [768], replicated
- grad_norm1_shift: float32 [768], replicated
- grad_up_weight: float32 [768, 3072], replicated
- grad_up_bias: float32 [3072], replicated
- grad_down_weight: float32 [3072, 768], replicated
- grad_down_bias: float32 [768], replicated
- grad_norm2_gain: float32 [768], replicated
- grad_norm2_shift: float32 [768], replicated
The draws below stay inside these ranges and needn't reach their ends.
Inputs may be any that keep to these rules, and one draw needn't show every extreme that they name: `segment_ids`: along a row the segment numbers never fall; every row of 512 positions holds exactly 32 segments, none empty. `segment_counts`: for each row, the number of positions that segment_ids gives each segment, in order of segment number; they sum to 512.
All inputs are finite; a program needn't handle non-finite values.
Results may differ from the reference program's by a relative error of at most 0.009.
Values may be sent and summed in bfloat16 or wider, within the bound.
No kernel may reach another device: no remote copies, remote signals or barrier semaphores. Data moves between devices by JAX's collectives and lax.ppermute only.
A program may use at most 256 MiB of HBM per device.

```python
import math
import jax
import jax.numpy as jnp
from jax import lax

D = 768
HEADS = 12
HEAD_DIM = 64
FF = 3072
LEN = 512
SEGS = 32
MICRO = 4
ROWS = 16


def segment_layout(key):
    row_keys = jax.random.split(jax.random.fold_in(key, 11), MICRO * ROWS)
    row_numbers = jnp.arange(MICRO * ROWS, dtype=jnp.int32)

    def one_row(row_key, row_number):
        random_cuts = jnp.sort(jax.random.permutation(row_key, LEN - 1)[:SEGS - 1] + 1).astype(jnp.int32)
        packed_cuts = jnp.arange(1, SEGS, dtype=jnp.int32)
        cut_points = jnp.where(row_number == 0, packed_cuts, random_cuts)
        edge_points = jnp.concatenate([jnp.zeros((1,), jnp.int32), cut_points, jnp.full((1,), LEN, jnp.int32)])
        positions = jnp.arange(LEN, dtype=jnp.int32)
        seg_numbers = jnp.sum((positions[:, None] >= cut_points[None, :]).astype(jnp.int32), axis=1)
        return (seg_numbers, edge_points[1:] - edge_points[:-1])
    seg_numbers, seg_sizes = jax.vmap(one_row)(row_keys, row_numbers)
    return (seg_numbers.reshape(MICRO, ROWS, LEN), seg_sizes.reshape(MICRO, ROWS, SEGS))


def draw_segment_ids(key, part):
    return segment_layout(key)[0]


def draw_segment_counts(key, part):
    return segment_layout(key)[1]


def shard_levels(own_key, extent, shards, smallest, top_value):
    factor_of = 1.0
    for position, shards_of in shards:
        draws = jax.random.uniform(jax.random.fold_in(jax.random.fold_in(own_key, 6), position), (shards_of,), jnp.float32, smallest / len(shards), top_value / len(shards))
        factor_of = factor_of * jnp.repeat(jnp.exp(draws), extent[position] // shards_of).reshape((-1,) + (1,) * (len(extent) - 1 - position))
    return factor_of


def noise(key, shape, width, bound, cuts=(), held_as=jnp.bfloat16):
    loudness = shard_levels(key, shape, cuts, -0.22, 0.18) if cuts else 1.0
    drawn = jax.random.normal(key, shape, jnp.float32) * width * loudness
    return jnp.minimum(jnp.maximum(drawn, -bound), bound).astype(held_as)


def setup_inputs(seed: int = 0) -> dict:
    keys = jax.random.split(jax.random.key(seed), 18)
    hidden_in = noise(keys[0], (MICRO, ROWS, LEN, D), 1.0, 6.0, ((1, 16), (2, 2)))
    segment_ids = draw_segment_ids(jax.random.fold_in(keys[17], 71), 0)
    segment_counts = draw_segment_counts(jax.random.fold_in(keys[17], 71), 0)
    pooled_grad = noise(keys[3], (MICRO, ROWS, SEGS, D), (LEN // SEGS), 96.0, ((1, 16),), jnp.float32)
    qkv_weight = noise(keys[4], (D, 3 * D), D ** -0.5, 0.21875)
    query_bias = noise(keys[5], (D,), 0.5, 3.0, (), jnp.float32)
    value_bias = noise(keys[6], (D,), 0.5, 3.0, (), jnp.float32)
    out_weight = noise(keys[7], (D, D), (D // 32) ** -0.5, 1.25)
    out_bias = noise(keys[8], (D,), 0.4, 2.5, (), jnp.float32)
    norm1_gain = jnp.clip(1.0 + 0.12 * jax.random.normal(keys[9], (D,), jnp.float32), 0.4, 1.6)
    norm1_shift = noise(keys[10], (D,), 0.4, 2.5, (), jnp.float32)
    up_weight = noise(keys[11], (D, FF), D ** -0.5, 0.21875)
    up_bias = noise(keys[12], (FF,), 0.5, 3.0, (), jnp.float32)
    down_weight = noise(keys[13], (FF, D), (FF // 2) ** -0.5, 0.15625)
    down_bias = noise(keys[14], (D,), 0.4, 2.5, (), jnp.float32)
    norm2_gain = jnp.clip(1.0 + 0.12 * jax.random.normal(keys[15], (D,), jnp.float32), 0.4, 1.6)
    norm2_shift = noise(keys[16], (D,), 0.4, 2.5, (), jnp.float32)
    return {"hidden_in": hidden_in, "segment_ids": segment_ids, "segment_counts": segment_counts, "pooled_grad": pooled_grad, "qkv_weight": qkv_weight, "query_bias": query_bias, "value_bias": value_bias, "out_weight": out_weight, "out_bias": out_bias, "norm1_gain": norm1_gain, "norm1_shift": norm1_shift, "up_weight": up_weight, "up_bias": up_bias, "down_weight": down_weight, "down_bias": down_bias, "norm2_gain": norm2_gain, "norm2_shift": norm2_shift}


NORM_EPS = 1e-05
MASK_FILL = -1e+30

@jax.custom_vjp
def low(v):
    return lax.optimization_barrier(v.astype(jnp.bfloat16)).astype(jnp.float32)

@jax.custom_vjp
def low_back(v):
    return v

def low_keep(v):
    return (low(v), None)

def low_pass(kept, grad):
    return (grad,)

def back_keep(v):
    return (v, None)

def back_low(kept, grad):
    return (low(grad),)
low.defvjp(low_keep, low_pass)
low_back.defvjp(back_keep, back_low)

def product(left_arg, right_arg):
    return jnp.dot(left_arg, right_arg, precision=lax.Precision.HIGHEST, preferred_element_type=jnp.float32)

def layer_norm(total_in, gain_vec, shift_vec):
    row_mean = lax.optimization_barrier(jnp.mean(total_in, axis=-1, keepdims=True))
    centered = total_in - row_mean
    variance = lax.optimization_barrier(jnp.mean(centered * centered, axis=-1, keepdims=True))
    return centered * lax.rsqrt(variance + NORM_EPS) * gain_vec + shift_vec

def forward(weights, tokens_in, seg_ids, seg_counts):
    qkv_weight, query_bias, value_bias, out_weight, out_bias, norm1_gain, norm1_shift, up_weight, up_bias, down_weight, down_bias, norm2_gain, norm2_shift = weights
    group_rows = tokens_in.shape[0]
    score_scale = HEAD_DIM ** (-0.5)
    flat_in = tokens_in.reshape(group_rows * LEN, D)
    shift_qkv = jnp.concatenate([query_bias, jnp.zeros((D,), jnp.float32), value_bias])
    qkv_proj = low(low_back(product(flat_in, qkv_weight) + shift_qkv))
    queries = qkv_proj[:, :D].reshape(group_rows, LEN, HEADS, HEAD_DIM)
    keys_heads = qkv_proj[:, D:2 * D].reshape(group_rows, LEN, HEADS, HEAD_DIM)
    values_heads = qkv_proj[:, 2 * D:].reshape(group_rows, LEN, HEADS, HEAD_DIM)
    raw_scores = low_back(jnp.einsum('gqhd,gkhd->ghqk', queries, keys_heads, precision=lax.Precision.HIGHEST) * score_scale)
    same_seg = (seg_ids[:, :, None] == seg_ids[:, None, :])[:, None]
    masked = jnp.where(same_seg, raw_scores, MASK_FILL)
    probs = low(jax.nn.softmax(masked, axis=-1))
    context = low(low_back(jnp.einsum('ghqk,gkhd->gqhd', probs, values_heads, precision=lax.Precision.HIGHEST).reshape(group_rows * LEN, D)))
    attn_out = low_back(product(context, out_weight) + out_bias)
    mid_out = layer_norm(flat_in + attn_out, norm1_gain, norm1_shift)
    up_pre = low_back(product(low(mid_out), up_weight) + up_bias)
    act_low = low(jax.nn.gelu(up_pre, approximate=False))
    down_out = low_back(product(act_low, down_weight) + down_bias)
    normed_out = layer_norm(mid_out + down_out, norm2_gain, norm2_shift)
    member = (seg_ids[..., None] == jnp.arange(SEGS, dtype=jnp.int32)).astype(jnp.float32)
    seg_sums = jnp.einsum('gts,gtd->gsd', member, normed_out.reshape(group_rows, LEN, D), precision=lax.Precision.HIGHEST)
    return seg_sums / seg_counts.astype(jnp.float32)[..., None]

def reference(hidden_in, segment_ids, segment_counts, pooled_grad, qkv_weight, query_bias, value_bias, out_weight, out_bias, norm1_gain, norm1_shift, up_weight, up_bias, down_weight, down_bias, norm2_gain, norm2_shift):
    weights = tuple((item_w.astype(jnp.float32) for item_w in (qkv_weight, query_bias, value_bias, out_weight, out_bias, norm1_gain, norm1_shift, up_weight, up_bias, down_weight, down_bias, norm2_gain, norm2_shift)))
    total_rows = MICRO * ROWS
    group_rows = math.gcd(total_rows, max(1, 4096 // LEN))
    blocks = total_rows // group_rows
    tokens_all = hidden_in.reshape(blocks, group_rows, LEN, D)
    ids_all = segment_ids.reshape(blocks, group_rows, LEN)
    counts_all = segment_counts.reshape(blocks, group_rows, SEGS)
    cotangent = pooled_grad.reshape(blocks, group_rows, SEGS, D)

    def scan_step(running, block_in):
        tokens_blk, ids_blk, counts_blk, cot_blk = block_in
        pooled_blk, pull_back = jax.vjp(lambda weight_set, tokens_f: forward(weight_set, tokens_f, ids_blk, counts_blk), weights, tokens_blk.astype(jnp.float32))
        grad_weights, grad_tokens = pull_back(cot_blk.astype(jnp.float32))
        running = tuple((a + b for a, b in zip(running, grad_weights)))
        return (running, (pooled_blk, grad_tokens.astype(jnp.bfloat16)))
    start_grads = tuple((jnp.zeros(item_w.shape, jnp.float32) for item_w in weights))
    summed, (pooled_all, grads_in) = lax.scan(scan_step, start_grads, (tokens_all, ids_all, counts_all, cotangent))
    pooled = pooled_all.reshape(MICRO, ROWS, SEGS, D)
    grad_input = grads_in.reshape(MICRO, ROWS, LEN, D)
    return (pooled, grad_input, summed[0], summed[1], summed[2], summed[3], summed[4], summed[5], summed[6], summed[7], summed[8], summed[9], summed[10], summed[11], summed[12])
```

```python
import jax
import jax.numpy as jnp
from jax import lax
from jax.sharding import PartitionSpec as P

D = 768
HEADS = 12
HEAD_DIM = 64
FF = 3072
SEGS = 32

NORM_EPS = 1e-05
MASK_FILL = -1e30
BF = jnp.bfloat16
F32 = jnp.float32


def norm_forward(total_in, gain_vec, shift_vec):
    row_mean = jnp.mean(total_in, axis=-1, keepdims=True)
    centered = total_in - row_mean
    inv_std = lax.rsqrt(jnp.mean(centered * centered, axis=-1, keepdims=True) + NORM_EPS)
    normed = centered * inv_std
    return (normed * gain_vec + shift_vec, normed, inv_std)


def norm_backward(grad_in, normed, inv_std, gain_vec):
    scaled = grad_in * gain_vec
    inner_part = (
        scaled
        - jnp.mean(scaled, axis=-1, keepdims=True)
        - normed * jnp.mean(scaled * normed, axis=-1, keepdims=True)
    )
    return (inner_part * inv_std, jnp.sum(grad_in * normed, axis=0), jnp.sum(grad_in, axis=0))


def weight_grad(left_arg, right_arg):
    return jnp.einsum("nd,nf->df", left_arg, right_arg, preferred_element_type=F32)


def back_product(grad_low, weight_mat):
    return jnp.einsum("nf,df->nd", grad_low, weight_mat, preferred_element_type=F32)


class Links:
    def __init__(self):
        self.dp = lax.axis_size("dp")
        self.seq = lax.axis_size("seq")
        dp_at = lax.axis_index("dp")
        seq_at = lax.axis_index("seq")
        core = dp_at % 2

        def flip(bit_of):
            pairs = []
            for d in range(self.dp):
                for s in range(self.seq):
                    bit = bit_of(d % 2)
                    to = (d, s ^ 1) if bit < 0 else (d ^ (1 << bit), s)
                    pairs.append((d * self.seq + s, to[0] * self.seq + to[1]))
            return pairs

        def side(bit):
            return seq_at if bit < 0 else (dp_at >> bit) % 2

        self.stages = [
            (flip(lambda c: 0), core),
            (flip(lambda c: 1 if c == 0 else -1), jnp.where(core == 0, side(1), side(-1))),
            (flip(lambda c: -1 if c == 0 else 1), jnp.where(core == 0, side(-1), side(1))),
        ]
        bits = (self.dp - 1).bit_length()
        for bit in range(2, bits):
            self.stages.append((flip(lambda c, bit=bit: bit), side(bit)))

    def scatter_sum(self, full):
        cur = full
        for pairs, at in self.stages:
            half = cur.shape[0] // 2
            send = lax.dynamic_slice_in_dim(cur, (1 - at) * half, half, 0).astype(BF)
            keep = lax.dynamic_slice_in_dim(cur, at * half, half, 0)
            recv = lax.ppermute(send, ("dp", "seq"), pairs)
            cur = keep.astype(F32) + recv.astype(F32)
        return cur.astype(BF)

    def gather(self, part):
        cur = part
        for pairs, at in reversed(self.stages):
            recv = lax.ppermute(cur, ("dp", "seq"), pairs)
            cur = jnp.where(at == 0, jnp.concatenate([cur, recv]), jnp.concatenate([recv, cur]))
        return cur


def swap_seq(value):
    return lax.ppermute(value, "seq", [(0, 1), (1, 0)])


def local(
    hidden_in,
    segment_ids,
    segment_counts,
    pooled_grad,
    qkv_weight,
    query_bias,
    value_bias,
    out_weight,
    out_bias,
    norm1_gain,
    norm1_shift,
    up_weight,
    up_bias,
    down_weight,
    down_bias,
    norm2_gain,
    norm2_shift,
):
    links = Links()
    seq_at = lax.axis_index("seq")
    micro, row_count, piece, _ = hidden_in.shape
    length = piece * 2
    own_micro = micro // 2
    rows = own_micro * row_count
    tokens = rows * length
    score_scale = HEAD_DIM ** (-0.5)

    def own_part(value):
        return lax.dynamic_slice_in_dim(value, seq_at * own_micro, own_micro, 0)

    def other_part(value):
        return lax.dynamic_slice_in_dim(value, (1 - seq_at) * own_micro, own_micro, 0)

    got = swap_seq(other_part(hidden_in))
    mine = own_part(hidden_in)
    full_rows = jnp.where(
        seq_at == 0,
        jnp.concatenate([mine, got], axis=2),
        jnp.concatenate([got, mine], axis=2),
    )
    flat_in = full_rows.reshape(tokens, D)
    counts = own_part(segment_counts).reshape(rows, SEGS)
    grads_pooled = own_part(pooled_grad).reshape(rows, SEGS, D)
    ends = jnp.sum(
        jnp.where(jnp.arange(SEGS)[None, :, None] <= jnp.arange(SEGS)[None, None, :], counts[:, :, None], 0),
        axis=1,
    )
    positions = jnp.arange(length, dtype=jnp.int32)
    ids = jnp.sum((positions[None, :, None] >= ends[:, None, :-1]).astype(jnp.int32), axis=-1)
    same_seg = ids[:, None, :, None] == ids[:, None, None, :]
    shift_qkv = jnp.concatenate([query_bias, jnp.zeros((D,), F32), value_bias])
    qkv_proj = (jnp.dot(flat_in, qkv_weight, preferred_element_type=F32) + shift_qkv).astype(BF)
    queries = qkv_proj[:, :D].reshape(rows, length, HEADS, HEAD_DIM)
    keys = qkv_proj[:, D : 2 * D].reshape(rows, length, HEADS, HEAD_DIM)
    values = qkv_proj[:, 2 * D :].reshape(rows, length, HEADS, HEAD_DIM)
    scores = jnp.where(
        same_seg,
        jnp.einsum("rqhd,rkhd->rhqk", queries, keys, preferred_element_type=F32) * score_scale,
        MASK_FILL,
    )
    row_max = jnp.max(scores, axis=-1, keepdims=True)
    exps = jnp.exp(scores - row_max)
    total_e = jnp.sum(exps, axis=-1, keepdims=True)
    log_total = row_max + jnp.log(total_e)
    probs_low = (exps / total_e).astype(BF)
    context = (
        jnp.einsum("rhqk,rkhd->rqhd", probs_low, values, preferred_element_type=F32)
        .reshape(tokens, D)
        .astype(BF)
    )
    attn_out = jnp.dot(context, out_weight, preferred_element_type=F32) + out_bias
    mid_out, normed1, inv_std1 = norm_forward(
        flat_in.astype(F32) + attn_out, norm1_gain, norm1_shift
    )
    mid_low = mid_out.astype(BF)
    up_pre = jnp.dot(mid_low, up_weight, preferred_element_type=F32) + up_bias
    cdf = 0.5 * (1.0 + lax.erf(up_pre * (0.5**0.5)))
    act_low = (up_pre * cdf).astype(BF)
    down_out = jnp.dot(act_low, down_weight, preferred_element_type=F32) + down_bias
    normed_out, normed2, inv_std2 = norm_forward(mid_out + down_out, norm2_gain, norm2_shift)
    member = (ids[..., None] == jnp.arange(SEGS, dtype=jnp.int32)).astype(F32)
    seg_size = counts.astype(F32)[..., None]
    pooled_own = (
        jnp.einsum(
            "rts,rtd->rsd",
            member,
            normed_out.reshape(rows, length, D),
            precision=lax.Precision.HIGHEST,
        )
        / seg_size
    ).reshape(own_micro, row_count, SEGS, D)
    pooled_got = swap_seq(pooled_own)
    pooled_local = jnp.where(
        seq_at == 0,
        jnp.concatenate([pooled_own, pooled_got]),
        jnp.concatenate([pooled_got, pooled_own]),
    )
    grad_out = jnp.einsum(
        "rts,rsd->rtd", member, grads_pooled / seg_size, precision=lax.Precision.HIGHEST
    ).reshape(tokens, D)
    grad_h2, grad_gain2, grad_shift2 = norm_backward(grad_out, normed2, inv_std2, norm2_gain)
    grad_down_low = grad_h2.astype(BF)
    grad_down_w = links.scatter_sum(weight_grad(act_low, grad_down_low).astype(BF))
    grad_down_b = jnp.sum(grad_down_low.astype(F32), axis=0)
    grad_act = back_product(grad_down_low, down_weight)
    slope = cdf + up_pre * (jnp.exp(-0.5 * up_pre * up_pre) * 0.3989422804014327)
    grad_up_low = (grad_act * slope).astype(BF)
    grad_up_w = links.scatter_sum(weight_grad(mid_low, grad_up_low).astype(BF))
    grad_up_b = jnp.sum(grad_up_low.astype(F32), axis=0)
    grad_mid = grad_h2 + back_product(grad_up_low, up_weight)
    grad_h1, grad_gain1, grad_shift1 = norm_backward(grad_mid, normed1, inv_std1, norm1_gain)
    grad_attn_low = grad_h1.astype(BF)
    grad_out_w = weight_grad(context, grad_attn_low).astype(BF)
    grad_out_b = jnp.sum(grad_attn_low.astype(F32), axis=0)
    grad_context = (
        back_product(grad_attn_low, out_weight).astype(BF).reshape(rows, length, HEADS, HEAD_DIM)
    )
    probs_back = jnp.exp(scores - log_total)
    probs_back_low = probs_back.astype(BF)
    grad_probs = jnp.einsum("rqhd,rkhd->rhqk", grad_context, values, preferred_element_type=F32)
    grad_scores = (
        probs_back * (grad_probs - jnp.sum(probs_back * grad_probs, axis=-1, keepdims=True))
    ).astype(BF)
    grad_queries = (
        jnp.einsum("rhqk,rkhd->rqhd", grad_scores, keys, preferred_element_type=F32) * score_scale
    )
    grad_keys = (
        jnp.einsum("rhqk,rqhd->rkhd", grad_scores, queries, preferred_element_type=F32) * score_scale
    )
    grad_values = jnp.einsum(
        "rhqk,rqhd->rkhd", probs_back_low, grad_context, preferred_element_type=F32
    )
    grad_qkv = jnp.concatenate(
        [
            grad_queries.reshape(tokens, D),
            grad_keys.reshape(tokens, D),
            grad_values.reshape(tokens, D),
        ],
        axis=1,
    ).astype(BF)
    grad_qkv_w = weight_grad(flat_in, grad_qkv).astype(BF)
    bias_sums = jnp.sum(grad_qkv.astype(F32), axis=0)
    grad_flat = (grad_h1 + back_product(grad_qkv, qkv_weight)).astype(BF)
    grad_rows = grad_flat.reshape(own_micro, row_count, length, D)
    back_own = lax.dynamic_slice_in_dim(grad_rows, seq_at * piece, piece, 2)
    back_got = swap_seq(lax.dynamic_slice_in_dim(grad_rows, (1 - seq_at) * piece, piece, 2))
    input_local = jnp.where(
        seq_at == 0, jnp.concatenate([back_own, back_got]), jnp.concatenate([back_got, back_own])
    )
    small = jnp.stack(
        [
            bias_sums[:D],
            bias_sums[2 * D :],
            grad_out_b,
            grad_gain1,
            grad_shift1,
            grad_down_b,
            grad_gain2,
            grad_shift2,
        ]
        + [grad_up_b[i * D : (i + 1) * D] for i in range(FF // D)],
        axis=1,
    )
    small = jnp.pad(small, ((0, 0), (0, 128 - small.shape[1]))).astype(BF)
    tail = links.scatter_sum(jnp.concatenate([grad_out_w, grad_qkv_w, small], axis=1))
    down_all = links.gather(grad_down_w).astype(F32)
    up_all = links.gather(grad_up_w).astype(F32)
    tail_all = links.gather(tail).astype(F32)
    small_all = tail_all[:, 4 * D :]
    return (
        pooled_local,
        input_local,
        tail_all[:, D : 4 * D],
        small_all[:, 0],
        small_all[:, 1],
        tail_all[:, :D],
        small_all[:, 2],
        small_all[:, 3],
        small_all[:, 4],
        up_all,
        small_all[:, 8 : 8 + FF // D].T.reshape(FF),
        down_all,
        small_all[:, 5],
        small_all[:, 6],
        small_all[:, 7],
    )


def solution(mesh):
    rep = P()
    in_specs = (
        P(None, "dp", "seq", None),
        P(None, "dp", "seq"),
        P(None, "dp", None),
        P(None, "dp", None, None),
    ) + (rep,) * 13
    out_specs = (P(None, "dp", None, None), P(None, "dp", "seq", None)) + (rep,) * 13
    return jax.shard_map(local, mesh=mesh, in_specs=in_specs, out_specs=out_specs, check_vma=False)
```

```python
import functools

import jax
import jax.numpy as jnp
from jax import lax
from jax.experimental import pallas as pl
from jax.experimental.pallas import tpu as pltpu
from jax.sharding import PartitionSpec as P

D = 768
HEADS = 12
HEAD_DIM = 64
FF = 3072
SEGS = 32
NORM_EPS = 1e-05
MASK_FILL = -1e30
BF = jnp.bfloat16
F32 = jnp.float32
VMEM_LIMIT = 60 * 1024 * 1024
PAIR = 2 * HEAD_DIM
STRIP = 128
CHUNK = 512
STAT_ROWS = 4 * HEADS

NN = (((1,), (0,)), ((), ()))
NT = (((1,), (1,)), ((), ()))
TN = (((0,), (0,)), ((), ()))


def mm(left, right, dims=NN):
    return lax.dot_general(left, right, dims, preferred_element_type=F32)


def whole(shape):
    zeros = (0,) * len(shape)
    return pl.BlockSpec(shape, lambda *_: zeros, pipeline_mode=pl.Buffered(1))


def params():
    return pltpu.CompilerParams(vmem_limit_bytes=VMEM_LIMIT)


def row_mean(value):
    return jnp.sum(value, axis=-1, keepdims=True) * (1.0 / D)


def attend_forward(at_ref, own_ref, got_ref, idc_ref, idr_ref, wqkv_ref, bqkv_ref, wo_ref, bo_ref, qkv_ref, xt_ref, ctxt_ref, lse_ref, xhat_ref, inv_ref, x_ref, ctx_ref, mask_ref, stat_ref):
    length = x_ref.shape[0]
    half = length // 2
    x_ref[pl.ds(pl.multiple_of(at_ref[0] * half, half), half), :] = own_ref[...]
    x_ref[pl.ds(pl.multiple_of((1 - at_ref[0]) * half, half), half), :] = got_ref[...]
    xt_ref[...] = jnp.transpose(x_ref[...])
    for c in range(3):
        cols = pl.ds(c * D, D)
        part = mm(x_ref[...], wqkv_ref[:, cols]) + bqkv_ref[:, cols]
        part = part.astype(BF)
        if c == 0:
            part = part * BF(HEAD_DIM**-0.5)
        qkv_ref[:, cols] = part
    mask_ref[...] = jnp.where(idc_ref[...] == idr_ref[...], 0.0, MASK_FILL)
    low = lax.broadcasted_iota(jnp.int32, (length, PAIR), 1) < HEAD_DIM
    low_strip = lax.broadcasted_iota(jnp.int32, (STRIP, PAIR), 1) < HEAD_DIM
    lane = lax.broadcasted_iota(jnp.int32, (STRIP, 128), 1)
    stat_ref[...] = jnp.zeros_like(stat_ref)

    def pair_step(p, carry):
        at = pl.multiple_of(p * PAIR, PAIR)
        keys = qkv_ref[:, pl.ds(D + at, PAIR)]
        values = qkv_ref[:, pl.ds(2 * D + at, PAIR)]
        value_of = [jnp.where(low, values, BF(0)), jnp.where(low, BF(0), values)]
        for s in range(length // STRIP):
            rows = pl.ds(s * STRIP, STRIP)
            queries = qkv_ref[rows, pl.ds(at, PAIR)]
            outs = []
            stats = stat_ref[rows, :]
            for h in range(2):
                query = jnp.where(low_strip, queries, BF(0)) if h == 0 else jnp.where(low_strip, BF(0), queries)
                scores = mm(query, keys, NT) + mask_ref[rows, :]
                top = jnp.max(scores, axis=-1, keepdims=True)
                exps = jnp.exp(scores - top)
                total = jnp.sum(exps, axis=-1, keepdims=True)
                outs.append(mm(exps.astype(BF), value_of[h]) * (1.0 / total))
                stats = jnp.where(lane == 8 * p + h, top + jnp.log(total), stats)
            ctx_ref[rows, pl.ds(at, PAIR)] = (outs[0] + outs[1]).astype(BF)
            stat_ref[rows, :] = stats
        return carry

    lax.fori_loop(0, HEADS // 2, pair_step, 0)
    lse_ref[...] = jnp.transpose(stat_ref[...])[: lse_ref.shape[0], :]
    ctxt_ref[...] = jnp.transpose(ctx_ref[...])
    total_in = mm(ctx_ref[...], wo_ref[...]) + bo_ref[...] + x_ref[...].astype(F32)
    centered = total_in - row_mean(total_in)
    inv = lax.rsqrt(row_mean(centered * centered) + NORM_EPS)
    xhat_ref[...] = centered * inv
    inv_ref[...] = jnp.broadcast_to(inv, inv_ref.shape)


def run_attend_forward(at, hidden, got, ids, wqkv, bqkv, wo, bo):
    rows, half, _ = got.shape
    length = 2 * half
    row_spec = lambda *tail: pl.BlockSpec((None,) + tail, lambda r, at: (r,) + (0,) * len(tail))
    turned = pl.BlockSpec((D, length), lambda r, at: (0, r))
    return pl.pallas_call(
        attend_forward,
        grid_spec=pltpu.PrefetchScalarGridSpec(
            num_scalar_prefetch=1,
            grid=(rows,),
            in_specs=[
                pl.BlockSpec((None, half, D), lambda r, at: (at[0] * rows + r, 0, 0)),
                row_spec(half, D), row_spec(length, 1), row_spec(1, length), whole((D, 3 * D)), whole((1, 3 * D)), whole((D, D)), whole((1, D))],
            out_specs=[row_spec(length, 3 * D), turned, turned, row_spec(STAT_ROWS, length), row_spec(length, D), row_spec(length, 128)],
            scratch_shapes=[pltpu.VMEM((length, D), BF), pltpu.VMEM((length, D), BF), pltpu.VMEM((length, length), F32), pltpu.VMEM((length, 128), F32)],
        ),
        out_shape=[
            jax.ShapeDtypeStruct((rows, length, 3 * D), BF),
            jax.ShapeDtypeStruct((D, rows * length), BF),
            jax.ShapeDtypeStruct((D, rows * length), BF),
            jax.ShapeDtypeStruct((rows, STAT_ROWS, length), F32),
            jax.ShapeDtypeStruct((rows, length, D), F32),
            jax.ShapeDtypeStruct((rows, length, 128), F32),
        ],
        compiler_params=params(),
        name="attend_forward",
    )(at, hidden, got, ids[:, :, None], ids[:, None, :], wqkv, bqkv[None], wo, bo[None])


def gelu_parts(value):
    cdf = 0.5 * (1.0 + lax.erf(value * (0.5**0.5)))
    density = jnp.exp(-0.5 * value * value) * 0.3989422804014327
    return cdf, cdf + value * density


def split_terms(value, count):
    parts = []
    for _ in range(count):
        part = value.astype(BF)
        parts.append(part)
        value = value - part.astype(F32)
    return parts


def feed_forward(xhat_ref, idc_ref, idr_ref, cnt_ref, pg_ref, g1_ref, s1_ref, up_ref, upb_ref, down_ref, downb_ref, g2_ref, s2_ref,
                 midt_ref, actt_ref, slope_ref, gh2_ref, gdl_ref, pooled_ref, sums_ref, mid_ref, acc_ref):
    length = xhat_ref.shape[0]
    mid = xhat_ref[...] * g1_ref[...] + s1_ref[...]
    mid_ref[...] = mid.astype(BF)
    midt_ref[...] = jnp.transpose(mid_ref[...])
    acc_ref[...] = mid + downb_ref[...]

    def chunk_step(c, carry):
        cols = pl.ds(pl.multiple_of(c * CHUNK, CHUNK), CHUNK)
        pre = mm(mid_ref[...], up_ref[:, cols]) + upb_ref[:, cols]
        cdf, slope = gelu_parts(pre)
        act = (pre * cdf).astype(BF)
        actt_ref[cols, :] = jnp.transpose(act)
        slope_ref[:, cols] = slope.astype(BF)
        acc_ref[...] += mm(act, down_ref[cols, :])
        return carry

    lax.fori_loop(0, FF // CHUNK, chunk_step, 0)
    total_in = acc_ref[...]
    centered = total_in - row_mean(total_in)
    inv = lax.rsqrt(row_mean(centered * centered) + NORM_EPS)
    normed = centered * inv
    final = normed * g2_ref[...] + s2_ref[...]
    member = (lax.broadcasted_iota(jnp.int32, (SEGS, length), 0) == idr_ref[...]).astype(BF)
    sums = sum(mm(member, part) for part in split_terms(final, 3))
    pooled_ref[...] = sums / cnt_ref[...]
    spread = (lax.broadcasted_iota(jnp.int32, (length, SEGS), 1) == idc_ref[...]).astype(BF)
    grad_final = sum(mm(spread, part) for part in split_terms(pg_ref[...] / cnt_ref[...], 3))
    scaled = grad_final * g2_ref[...]
    grad_h2 = inv * (scaled - row_mean(scaled) - normed * row_mean(scaled * normed))
    gh2_ref[...] = grad_h2
    low = grad_h2.astype(BF)
    gdl_ref[...] = low
    sums_ref[0:1, :] = jnp.sum(grad_final * normed, axis=0, keepdims=True)
    sums_ref[1:2, :] = jnp.sum(grad_final, axis=0, keepdims=True)
    sums_ref[2:3, :] = jnp.sum(low.astype(F32), axis=0, keepdims=True)
    sums_ref[3:8, :] = jnp.zeros((5, D), F32)


def run_feed_forward(xhat, ids, counts, pooled_grad, g1, s1, up, upb, down, downb, g2, s2):
    rows, length, _ = xhat.shape
    row_spec = lambda *tail: pl.BlockSpec((None,) + tail, lambda r: (r,) + (0,) * len(tail))
    return pl.pallas_call(
        feed_forward,
        grid=(rows,),
        in_specs=[row_spec(length, D), row_spec(length, 1), row_spec(1, length), row_spec(SEGS, 1), row_spec(SEGS, D), whole((1, D)), whole((1, D)),
                  whole((D, FF)), whole((1, FF)), whole((FF, D)), whole((1, D)), whole((1, D)), whole((1, D))],
        out_specs=[pl.BlockSpec((D, length), lambda r: (0, r)), pl.BlockSpec((FF, length), lambda r: (0, r)), row_spec(length, FF), row_spec(length, D), row_spec(length, D), row_spec(SEGS, D), row_spec(8, D)],
        out_shape=[
            jax.ShapeDtypeStruct((D, rows * length), BF),
            jax.ShapeDtypeStruct((FF, rows * length), BF),
            jax.ShapeDtypeStruct((rows, length, FF), BF),
            jax.ShapeDtypeStruct((rows, length, D), F32),
            jax.ShapeDtypeStruct((rows, length, D), BF),
            jax.ShapeDtypeStruct((rows, SEGS, D), F32),
            jax.ShapeDtypeStruct((rows, 8, D), F32),
        ],
        scratch_shapes=[pltpu.VMEM((length, D), BF), pltpu.VMEM((length, D), F32)],
        compiler_params=params(),
        name="feed_forward",
    )(xhat, ids[:, :, None], ids[:, None, :], counts.astype(F32)[:, :, None], pooled_grad, g1[None], s1[None], up, upb[None], down, downb[None], g2[None], s2[None])


def feed_backward(gdl_ref, slope_ref, gh2_ref, xhat_ref, inv_ref, g1_ref, up_ref, down_ref, gul_ref, gh1_ref, gal_ref, sums_ref, upsum_ref, acc_ref):
    acc_ref[...] = gh2_ref[...]

    def chunk_step(c, carry):
        cols = pl.ds(pl.multiple_of(c * CHUNK, CHUNK), CHUNK)
        grad_act = mm(gdl_ref[...], down_ref[cols, :], NT)
        low = (grad_act * slope_ref[:, cols].astype(F32)).astype(BF)
        gul_ref[:, cols] = low
        upsum_ref[0:1, cols] = jnp.sum(low.astype(F32), axis=0, keepdims=True)
        acc_ref[...] += mm(low, up_ref[:, cols], NT)
        return carry

    lax.fori_loop(0, FF // CHUNK, chunk_step, 0)
    grad_mid = acc_ref[...]
    normed = xhat_ref[...]
    scaled = grad_mid * g1_ref[...]
    inv = inv_ref[:, 0:1]
    grad_h1 = inv * (scaled - row_mean(scaled) - normed * row_mean(scaled * normed))
    gh1_ref[...] = grad_h1
    low = grad_h1.astype(BF)
    gal_ref[...] = low
    sums_ref[0:1, :] = jnp.sum(grad_mid * normed, axis=0, keepdims=True)
    sums_ref[1:2, :] = jnp.sum(grad_mid, axis=0, keepdims=True)
    sums_ref[2:3, :] = jnp.sum(low.astype(F32), axis=0, keepdims=True)
    sums_ref[3:8, :] = jnp.zeros((5, D), F32)


def run_feed_backward(gdl, slope, gh2, xhat, inv, g1, up, down):
    rows, length, _ = gdl.shape
    row_spec = lambda *tail: pl.BlockSpec((None,) + tail, lambda r: (r,) + (0,) * len(tail))
    return pl.pallas_call(
        feed_backward,
        grid=(rows,),
        in_specs=[row_spec(length, D), row_spec(length, FF), row_spec(length, D), row_spec(length, D), row_spec(length, 128), whole((1, D)), whole((D, FF)), whole((FF, D))],
        out_specs=[row_spec(length, FF), row_spec(length, D), row_spec(length, D), row_spec(8, D), row_spec(1, FF)],
        out_shape=[
            jax.ShapeDtypeStruct((rows, length, FF), BF),
            jax.ShapeDtypeStruct((rows, length, D), F32),
            jax.ShapeDtypeStruct((rows, length, D), BF),
            jax.ShapeDtypeStruct((rows, 8, D), F32),
            jax.ShapeDtypeStruct((rows, 1, FF), F32),
        ],
        scratch_shapes=[pltpu.VMEM((length, D), F32)],
        compiler_params=params(),
        name="feed_backward",
    )(gdl, slope, gh2, xhat, inv, g1[None], up, down)


def attend_backward(at_ref, gal_ref, gh1_ref, qkv_ref, lse_ref, idc_ref, idr_ref, wo_ref, wqkv_ref, gqkv_ref, own_ref, send_ref, sums_ref, mask_ref, gctx_ref):
    length = gal_ref.shape[0]
    gctx_ref[...] = mm(gal_ref[...], wo_ref[...], NT).astype(BF)
    mask_ref[...] = jnp.where(idc_ref[...] == idr_ref[...], 0.0, MASK_FILL)
    low_strip = lax.broadcasted_iota(jnp.int32, (STRIP, PAIR), 1) < HEAD_DIM
    low = lax.broadcasted_iota(jnp.int32, (length, PAIR), 1) < HEAD_DIM

    def pair_step(p, carry):
        at = pl.multiple_of(p * PAIR, PAIR)
        keys = qkv_ref[:, pl.ds(D + at, PAIR)]
        values = qkv_ref[:, pl.ds(2 * D + at, PAIR)]
        key_of = [jnp.where(low, keys, BF(0)), jnp.where(low, BF(0), keys)]
        grad_k = jnp.zeros((length, PAIR), F32)
        grad_v = jnp.zeros((length, PAIR), F32)
        for s in range(length // STRIP):
            rows = pl.ds(s * STRIP, STRIP)
            lses = lse_ref[pl.ds(pl.multiple_of(8 * p, 8), 8), rows]
            queries = qkv_ref[rows, pl.ds(at, PAIR)]
            grads = gctx_ref[rows, pl.ds(at, PAIR)]
            grad_q = jnp.zeros((STRIP, PAIR), F32)
            for h in range(2):
                pick = (lambda v: jnp.where(low_strip, v, BF(0))) if h == 0 else (lambda v: jnp.where(low_strip, BF(0), v))
                query, grad = pick(queries), pick(grads)
                scores = mm(keys, query, NT) + mask_ref[:, rows]
                probs = jnp.exp(scores - lses[h : h + 1, :])
                grad_p = mm(values, grad, NT)
                inner = jnp.sum(probs * grad_p, axis=0, keepdims=True)
                grad_s = (probs * (grad_p - inner)).astype(BF)
                grad_v += mm(probs.astype(BF), grad)
                grad_k += mm(grad_s, query)
                grad_q += mm(grad_s, key_of[h], TN)
            low_q = (grad_q * HEAD_DIM**-0.5).astype(BF)
            gqkv_ref[rows, pl.ds(at, PAIR)] = low_q
        gqkv_ref[:, pl.ds(D + at, PAIR)] = grad_k.astype(BF)
        gqkv_ref[:, pl.ds(2 * D + at, PAIR)] = grad_v.astype(BF)
        return carry

    lax.fori_loop(0, HEADS // 2, pair_step, 0)
    half = length // 2
    for out, first in ((own_ref, at_ref[0]), (send_ref, 1 - at_ref[0])):
        rows = pl.ds(pl.multiple_of(first * half, half), half)
        out[...] = (gh1_ref[rows, :] + mm(gqkv_ref[rows, :], wqkv_ref[...], NT)).astype(BF)
    sums_ref[...] = jnp.sum(gqkv_ref[...].astype(F32), axis=0, keepdims=True)


def run_attend_backward(at, gal, gh1, qkv, lse, ids, wo, wqkv):
    rows, length, _ = gal.shape
    half = length // 2
    row_spec = lambda *tail: pl.BlockSpec((None,) + tail, lambda r, at: (r,) + (0,) * len(tail))
    return pl.pallas_call(
        attend_backward,
        grid_spec=pltpu.PrefetchScalarGridSpec(
            num_scalar_prefetch=1,
            grid=(rows,),
            in_specs=[row_spec(length, D), row_spec(length, D), row_spec(length, 3 * D), row_spec(STAT_ROWS, length), row_spec(length, 1), row_spec(1, length), whole((D, D)), whole((D, 3 * D))],
            out_specs=[row_spec(length, 3 * D), row_spec(half, D), row_spec(half, D), row_spec(1, 3 * D)],
            scratch_shapes=[pltpu.VMEM((length, length), F32), pltpu.VMEM((length, D), BF)],
        ),
        out_shape=[
            jax.ShapeDtypeStruct((rows, length, 3 * D), BF),
            jax.ShapeDtypeStruct((rows, half, D), BF),
            jax.ShapeDtypeStruct((rows, half, D), BF),
            jax.ShapeDtypeStruct((rows, 1, 3 * D), F32),
        ],
        compiler_params=params(),
        name="attend_backward",
    )(at, gal, gh1, qkv, lse, ids[:, :, None], ids[:, None, :], wo, wqkv)


def grad_send(sides_ref, left_ref, right_ref, out_ref):
    out_ref[...] = mm(left_ref[...], right_ref[...]).astype(BF)


def grad_keep(sides_ref, left_send_ref, left_keep_ref, right_ref, got_send_ref, got_keep_ref, send_ref, keep_ref):
    right = right_ref[...]
    send_ref[...] = (mm(left_send_ref[...], right) + got_send_ref[...].astype(F32)).astype(BF)
    keep_ref[...] = mm(left_keep_ref[...], right) + got_keep_ref[...].astype(F32)


BLOCK = 384


def down_send(sides, left, right):
    total, width = left.shape[0], right.shape[1]
    steps = total // 2 // BLOCK
    return pl.pallas_call(
        grad_send,
        grid_spec=pltpu.PrefetchScalarGridSpec(
            num_scalar_prefetch=1,
            grid=(steps,),
            in_specs=[pl.BlockSpec((BLOCK, left.shape[1]), lambda i, sd: ((1 - sd[0]) * steps + i, 0)), whole(right.shape)],
            out_specs=pl.BlockSpec((BLOCK, width), lambda i, sd: (i, 0)),
        ),
        out_shape=jax.ShapeDtypeStruct((total // 2, width), BF),
        compiler_params=params(),
        name="down_send",
    )(sides, left, right)


def down_keep(sides, left, right, got):
    total, width = left.shape[0], right.shape[1]
    steps = total // 4 // BLOCK
    left_at = lambda part: pl.BlockSpec((BLOCK, left.shape[1]), lambda i, sd: ((2 * sd[0] + part(sd[1])) * steps + i, 0))
    got_at = lambda part: pl.BlockSpec((BLOCK, width), lambda i, sd: (part(sd[1]) * steps + i, 0))
    away, here = (lambda side: 1 - side), (lambda side: side)
    return pl.pallas_call(
        grad_keep,
        grid_spec=pltpu.PrefetchScalarGridSpec(
            num_scalar_prefetch=1,
            grid=(steps,),
            in_specs=[left_at(away), left_at(here), whole(right.shape), got_at(away), got_at(here)],
            out_specs=[pl.BlockSpec((BLOCK, width), lambda i, sd: (i, 0))] * 2,
        ),
        out_shape=[jax.ShapeDtypeStruct((total // 4, width), BF), jax.ShapeDtypeStruct((total // 4, width), F32)],
        compiler_params=params(),
        name="down_keep",
    )(sides, left, left, right, got, got)


def up_send_body(steps, sides_ref, mid_ref, gul_ref, ctx_ref, gal_ref, out_ref):
    @pl.when(pl.program_id(0) < steps)
    def _():
        out_ref[...] = mm(mid_ref[...], gul_ref[...]).astype(BF)

    @pl.when(pl.program_id(0) == steps)
    def _():
        out_ref[...] = mm(ctx_ref[...], gal_ref[...]).astype(BF)


def up_send(sides, mid, gul, ctx, gal):
    steps, half, tokens = FF // D, D // 2, mid.shape[1]
    return pl.pallas_call(
        functools.partial(up_send_body, steps),
        grid_spec=pltpu.PrefetchScalarGridSpec(
            num_scalar_prefetch=1,
            grid=(steps + 1,),
            in_specs=[
                pl.BlockSpec((half, tokens), lambda j, sd: (1 - sd[0], 0)),
                pl.BlockSpec((tokens, D), lambda j, sd: (0, jnp.minimum(j, steps - 1))),
                pl.BlockSpec((half, tokens), lambda j, sd: (1 - sd[0], 0)),
                whole(gal.shape),
            ],
            out_specs=pl.BlockSpec((half, D), lambda j, sd: (0, j)),
        ),
        out_shape=jax.ShapeDtypeStruct((half, FF + D), BF),
        compiler_params=params(),
        name="up_send",
    )(sides, mid, gul, ctx, gal)


def up_keep_body(steps, sides_ref, mid_send_ref, mid_keep_ref, gul_ref, ctx_send_ref, ctx_keep_ref, gal_ref, got_send_ref, got_keep_ref, send_ref, keep_ref):
    @pl.when(pl.program_id(0) < steps)
    def _():
        send_ref[...] = (mm(mid_send_ref[...], gul_ref[...]) + got_send_ref[...].astype(F32)).astype(BF)
        keep_ref[...] = mm(mid_keep_ref[...], gul_ref[...]) + got_keep_ref[...].astype(F32)

    @pl.when(pl.program_id(0) == steps)
    def _():
        send_ref[...] = (mm(ctx_send_ref[...], gal_ref[...]) + got_send_ref[...].astype(F32)).astype(BF)
        keep_ref[...] = mm(ctx_keep_ref[...], gal_ref[...]) + got_keep_ref[...].astype(F32)


def up_keep(sides, mid, gul, ctx, gal, got):
    steps, quarter, tokens = FF // D, D // 4, mid.shape[1]
    away, here = (lambda side: 1 - side), (lambda side: side)
    left_at = lambda part: pl.BlockSpec((quarter, tokens), lambda j, sd: (2 * sd[0] + part(sd[1]), 0))
    got_at = lambda part: pl.BlockSpec((quarter, D), lambda j, sd: (part(sd[1]), j))
    return pl.pallas_call(
        functools.partial(up_keep_body, steps),
        grid_spec=pltpu.PrefetchScalarGridSpec(
            num_scalar_prefetch=1,
            grid=(steps + 1,),
            in_specs=[
                left_at(away), left_at(here), pl.BlockSpec((tokens, D), lambda j, sd: (0, jnp.minimum(j, steps - 1))),
                left_at(away), left_at(here), whole(gal.shape), got_at(away), got_at(here),
            ],
            out_specs=[pl.BlockSpec((quarter, D), lambda j, sd: (0, j))] * 2,
        ),
        out_shape=[jax.ShapeDtypeStruct((quarter, FF + D), BF), jax.ShapeDtypeStruct((quarter, FF + D), F32)],
        compiler_params=params(),
        name="up_keep",
    )(sides, mid, mid, gul, ctx, ctx, gal, got, got)


SMALLS = 128


def gather_small(sums1_ref, sums2_ref, ups_ref, sq_ref, small_ref, pack_ref):
    pack_ref[...] = jnp.zeros_like(pack_ref)
    total = lambda ref: jnp.sum(ref[...], axis=0)
    first, second, ups, sq = total(sums1_ref), total(sums2_ref), total(ups_ref), total(sq_ref)
    lines = [sq[:, :D], sq[:, 2 * D :], first[2:3], first[0:1], first[1:2], second[2:3], second[0:1], second[1:2]]
    lines += [ups[:, i * D : (i + 1) * D] for i in range(FF // D)]
    for i, line in enumerate(lines):
        pack_ref[i : i + 1, :] = line
    small_ref[...] = jnp.transpose(pack_ref[...])


def tail_send_body(sides_ref, x_ref, gqkv_ref, sums1_ref, sums2_ref, ups_ref, sq_ref, out_ref, small_ref, pack_ref):
    half = x_ref.shape[0]
    gather_small(sums1_ref, sums2_ref, ups_ref, sq_ref, small_ref, pack_ref)
    out_ref[:, : 3 * D] = mm(x_ref[...], gqkv_ref[...]).astype(BF)
    rows = pl.ds(pl.multiple_of((1 - sides_ref[0]) * half, half), half)
    out_ref[:, 3 * D :] = small_ref[rows, :].astype(BF)


def tail_send(sides, x, gqkv, smalls):
    half, tokens = D // 2, x.shape[1]
    return pl.pallas_call(
        tail_send_body,
        grid_spec=pltpu.PrefetchScalarGridSpec(
            num_scalar_prefetch=1,
            grid=(1,),
            in_specs=[pl.BlockSpec((half, tokens), lambda j, sd: (1 - sd[0], 0)), whole(gqkv.shape)] + [whole(v.shape) for v in smalls],
            out_specs=pl.BlockSpec((half, 3 * D + SMALLS), lambda j, sd: (0, 0)),
            scratch_shapes=[pltpu.VMEM((D, SMALLS), F32), pltpu.VMEM((SMALLS, D), F32)],
        ),
        out_shape=jax.ShapeDtypeStruct((half, 3 * D + SMALLS), BF),
        compiler_params=params(),
        name="tail_send",
    )(sides, x, gqkv, *smalls)


def tail_keep_body(sides_ref, x_send_ref, x_keep_ref, gqkv_ref, sums1_ref, sums2_ref, ups_ref, sq_ref, got_send_ref, got_keep_ref, send_ref, keep_ref, small_ref, pack_ref):
    quarter = x_send_ref.shape[0]
    gather_small(sums1_ref, sums2_ref, ups_ref, sq_ref, small_ref, pack_ref)
    for left, got, out, side in ((x_send_ref, got_send_ref, send_ref, 1 - sides_ref[1]), (x_keep_ref, got_keep_ref, keep_ref, sides_ref[1])):
        rows = pl.ds(pl.multiple_of((2 * sides_ref[0] + side) * quarter, quarter), quarter)
        out[:, : 3 * D] = (mm(left[...], gqkv_ref[...]) + got[:, : 3 * D].astype(F32)).astype(out.dtype)
        out[:, 3 * D :] = (small_ref[rows, :] + got[:, 3 * D :].astype(F32)).astype(out.dtype)


def tail_keep(sides, x, gqkv, smalls, got):
    quarter, tokens, width = D // 4, x.shape[1], 3 * D + SMALLS
    away, here = (lambda side: 1 - side), (lambda side: side)
    left_at = lambda part: pl.BlockSpec((quarter, tokens), lambda j, sd: (2 * sd[0] + part(sd[1]), 0))
    got_at = lambda part: pl.BlockSpec((quarter, width), lambda j, sd: (part(sd[1]), 0))
    return pl.pallas_call(
        tail_keep_body,
        grid_spec=pltpu.PrefetchScalarGridSpec(
            num_scalar_prefetch=1,
            grid=(1,),
            in_specs=[left_at(away), left_at(here), whole(gqkv.shape)] + [whole(v.shape) for v in smalls] + [got_at(away), got_at(here)],
            out_specs=[pl.BlockSpec((quarter, width), lambda j, sd: (0, 0))] * 2,
            scratch_shapes=[pltpu.VMEM((D, SMALLS), F32), pltpu.VMEM((SMALLS, D), F32)],
        ),
        out_shape=[jax.ShapeDtypeStruct((quarter, width), BF), jax.ShapeDtypeStruct((quarter, width), F32)],
        compiler_params=params(),
        name="tail_keep",
    )(sides, x, x, gqkv, *smalls, got, got)


def add_split_body(at_ref, keep_away_ref, keep_here_ref, got_away_ref, got_here_ref, send_ref, next_ref):
    send_ref[...] = (keep_away_ref[...] + got_away_ref[...].astype(F32)).astype(BF)
    next_ref[...] = keep_here_ref[...] + got_here_ref[...].astype(F32)


def add_split(at, keep, got):
    half, width = keep.shape[0] // 2, keep.shape[1]
    cols = width // 2 if width % 256 == 0 else width
    away = pl.BlockSpec((half, cols), lambda j, at: (1 - at[0], j))
    here = pl.BlockSpec((half, cols), lambda j, at: (at[0], j))
    return pl.pallas_call(
        add_split_body,
        grid_spec=pltpu.PrefetchScalarGridSpec(
            num_scalar_prefetch=1,
            grid=(width // cols,),
            in_specs=[away, here, away, here],
            out_specs=[pl.BlockSpec((half, cols), lambda j, at: (0, j))] * 2,
        ),
        out_shape=[jax.ShapeDtypeStruct((half, width), BF), jax.ShapeDtypeStruct((half, width), F32)],
        compiler_params=params(),
        name="add_split",
    )(at, keep, keep, got, got)


def assemble_body(steps, widths, place_ref, *refs):
    pieces, outs = refs[:4], refs[4:]
    at = pl.program_id(0) // steps
    for p in range(4):

        @pl.when(at == p)
        def _(p=p):
            start = 0
            for out, width in zip(outs, widths):
                out[...] = pieces[p][:, start : start + width].astype(F32)
                start += width


def assemble(places, pieces, widths):
    quarter, width = pieces[0].shape
    block = min(quarter, 96)
    steps = quarter // block
    return pl.pallas_call(
        functools.partial(assemble_body, steps, widths),
        grid_spec=pltpu.PrefetchScalarGridSpec(
            num_scalar_prefetch=1,
            grid=(4 * steps,),
            in_specs=[pl.BlockSpec((block, width), lambda i, pos, p=p: (jnp.clip(i - p * steps, 0, steps - 1), 0)) for p in range(4)],
            out_specs=[pl.BlockSpec((block, w), lambda i, pos: (pos[i // steps] * steps + i % steps, 0)) for w in widths],
        ),
        out_shape=[jax.ShapeDtypeStruct((4 * quarter, w), F32) for w in widths],
        compiler_params=params(),
        name="assemble",
    )(places, *pieces)


class Links:
    def __init__(self):
        dp, seq = lax.axis_size("dp"), lax.axis_size("seq")
        dp_at, seq_at = lax.axis_index("dp"), lax.axis_index("seq")
        self.core = dp_at % 2

        def flip(bit_of):
            pairs = []
            for d in range(dp):
                for s in range(seq):
                    bit = bit_of(d % 2)
                    to = (d, s ^ 1) if bit < 0 else (d ^ (1 << bit), s)
                    pairs.append((d * seq + s, to[0] * seq + to[1]))
            return pairs

        second = (dp_at >> 1) % 2
        self.side_a = jnp.where(self.core == 0, second, seq_at)
        self.side_b = jnp.where(self.core == 0, seq_at, second)
        self.pairs_core = flip(lambda c: 0)
        self.pairs_a = flip(lambda c: 1 if c == 0 else -1)
        self.pairs_b = flip(lambda c: -1 if c == 0 else 1)
        self.rest = [(flip(lambda c, bit=bit: bit), (dp_at >> bit) % 2) for bit in range(2, (dp - 1).bit_length())]
        self.sides = jnp.stack([self.core, self.side_a]).astype(jnp.int32)
        self.side_b_array = self.side_b.astype(jnp.int32).reshape(1)
        other = 2 * (1 - self.core)
        mine = 2 * self.core
        self.places = jnp.stack([mine + self.side_a, mine + 1 - self.side_a, other + self.side_b, other + 1 - self.side_b]).astype(jnp.int32)

    def send(self, value, pairs):
        return lax.ppermute(value, ("dp", "seq"), pairs)

    def reduce_rest(self, keep, got):
        cur = keep + got.astype(F32)
        for pairs, at in self.rest:
            half = cur.shape[0] // 2
            away = lax.dynamic_slice_in_dim(cur, (1 - at) * half, half, 0).astype(BF)
            cur = lax.dynamic_slice_in_dim(cur, at * half, half, 0) + self.send(away, pairs).astype(F32)
        return cur.astype(BF)

    def spread_rest(self, part):
        cur = part
        for pairs, at in reversed(self.rest):
            got = self.send(cur, pairs)
            cur = jnp.where(at == 0, jnp.concatenate([cur, got]), jnp.concatenate([got, cur]))
        return cur

    def finish(self, away, keep, widths):
        got = self.send(away, self.pairs_a)
        away, keep = add_split(self.side_b_array, keep, got)
        got = self.send(away, self.pairs_b)
        part = self.reduce_rest(keep, got)
        cur = self.spread_rest(part)
        got = self.send(cur, self.pairs_b)
        quarter = jnp.where(self.side_b == 0, jnp.concatenate([cur, got]), jnp.concatenate([got, cur]))
        got = self.send(quarter, self.pairs_a)
        pieces = [quarter, got, self.send(quarter, self.pairs_core), self.send(got, self.pairs_core)]
        return assemble(self.places, pieces, widths)


def swap_seq(value):
    return lax.ppermute(value, "seq", [(0, 1), (1, 0)])


def local(
    hidden_in,
    segment_ids,
    segment_counts,
    pooled_grad,
    qkv_weight,
    query_bias,
    value_bias,
    out_weight,
    out_bias,
    norm1_gain,
    norm1_shift,
    up_weight,
    up_bias,
    down_weight,
    down_bias,
    norm2_gain,
    norm2_shift,
):
    links = Links()
    seq_at = lax.axis_index("seq")
    seq_array = seq_at.astype(jnp.int32).reshape(1)
    micro, row_count, piece, _ = hidden_in.shape
    length = piece * 2
    own_micro = micro // 2
    rows = own_micro * row_count
    tokens = rows * length

    def own_part(value):
        return lax.dynamic_slice_in_dim(value, seq_at * own_micro, own_micro, 0)

    got = swap_seq(lax.dynamic_slice_in_dim(hidden_in, (1 - seq_at) * own_micro, own_micro, 0))
    counts = own_part(segment_counts).reshape(rows, SEGS)
    pooled_cot = own_part(pooled_grad).reshape(rows, SEGS, D)
    seg = jnp.arange(SEGS, dtype=jnp.int32)
    ends = jnp.sum(jnp.where(seg[None, :, None] <= seg[None, None, :], counts[:, :, None], 0), axis=1)
    positions = jnp.arange(length, dtype=jnp.int32)
    ids = jnp.sum((positions[None, :, None] >= ends[:, None, :-1]).astype(jnp.int32), axis=-1)
    shift_qkv = jnp.concatenate([query_bias, jnp.zeros((D,), F32), value_bias])

    qkv, x_turned, ctx_turned, lse, xhat, inv = run_attend_forward(
        seq_array,
        hidden_in.reshape(micro * row_count, piece, D),
        got.reshape(rows, piece, D),
        ids,
        qkv_weight,
        shift_qkv,
        out_weight,
        out_bias,
    )
    mid_turned, act_turned, slope, grad_h2, grad_down_low, pooled, sums2 = run_feed_forward(
        xhat, ids, counts, pooled_cot, norm1_gain, norm1_shift, up_weight, up_bias, down_weight, down_bias, norm2_gain, norm2_shift
    )
    flat_down = grad_down_low.reshape(tokens, D)
    got_down = links.send(down_send(links.sides, act_turned, flat_down), links.pairs_core)
    pooled_own = pooled.reshape(own_micro, row_count, SEGS, D)
    pooled_got = swap_seq(pooled_own)
    pooled_local = jnp.where(
        seq_at == 0, jnp.concatenate([pooled_own, pooled_got]), jnp.concatenate([pooled_got, pooled_own])
    )
    grad_up_low, grad_h1, grad_attn_low, sums1, ups = run_feed_backward(
        grad_down_low, slope, grad_h2, xhat, inv, norm1_gain, up_weight, down_weight
    )
    away_down, keep_down = down_keep(links.sides, act_turned, flat_down, got_down)
    flat_up, flat_attn = grad_up_low.reshape(tokens, FF), grad_attn_low.reshape(tokens, D)
    got_up = links.send(up_send(links.sides, mid_turned, flat_up, ctx_turned, flat_attn), links.pairs_core)
    away_up, keep_up = up_keep(links.sides, mid_turned, flat_up, ctx_turned, flat_attn, got_up)
    grad_qkv, back_own, back_send, sums_qkv = run_attend_backward(
        seq_array, grad_attn_low, grad_h1, qkv, lse, ids, out_weight, qkv_weight
    )
    back_own = back_own.reshape(own_micro, row_count, piece, D)
    back_got = swap_seq(back_send.reshape(own_micro, row_count, piece, D))
    input_local = jnp.where(
        seq_at == 0, jnp.concatenate([back_own, back_got]), jnp.concatenate([back_got, back_own])
    )
    smalls = (sums1, sums2, ups, sums_qkv)
    flat_qkv = grad_qkv.reshape(tokens, 3 * D)
    got_tail = links.send(tail_send(links.sides, x_turned, flat_qkv, smalls), links.pairs_core)
    away_tail, keep_tail = tail_keep(links.sides, x_turned, flat_qkv, smalls, got_tail)
    (down_all,) = links.finish(away_down, keep_down, (D,))
    up_all, out_all = links.finish(away_up, keep_up, (FF, D))
    qkv_all, small_all = links.finish(away_tail, keep_tail, (3 * D, SMALLS))
    lines = small_all[:, : 8 + FF // D].T
    return (
        pooled_local,
        input_local,
        qkv_all,
        lines[0],
        lines[1],
        out_all,
        lines[2],
        lines[3],
        lines[4],
        up_all,
        lines[8 : 8 + FF // D].reshape(FF),
        down_all,
        lines[5],
        lines[6],
        lines[7],
    )


def solution(mesh):
    rep = P()
    in_specs = (
        P(None, "dp", "seq", None),
        P(None, "dp", "seq"),
        P(None, "dp", None),
        P(None, "dp", None, None),
    ) + (rep,) * 13
    out_specs = (P(None, "dp", None, None), P(None, "dp", "seq", None)) + (rep,) * 13
    return jax.shard_map(local, mesh=mesh, in_specs=in_specs, out_specs=out_specs, check_vma=False)
```

```python
import functools

import jax
import jax.numpy as jnp
from jax import lax
from jax.experimental import pallas as pl
from jax.experimental.pallas import tpu as pltpu
from jax.sharding import PartitionSpec as P

D = 768
HEADS = 12
HEAD_DIM = 64
FF = 3072
SEGS = 32
NORM_EPS = 1e-05
MASK_FILL = -1e30
BF = jnp.bfloat16
F32 = jnp.float32
PAIR = 2 * HEAD_DIM
STRIP = 512
CHUNK = 1024
STAT_ROWS = 4 * HEADS

NN = (((1,), (0,)), ((), ()))
NT = (((1,), (1,)), ((), ()))
TN = (((0,), (0,)), ((), ()))


def mm(left, right, dims=NN):
    return lax.dot_general(left, right, dims, preferred_element_type=F32)


def whole(shape):
    zeros = (0,) * len(shape)
    return pl.BlockSpec(shape, lambda *_: zeros, pipeline_mode=pl.Buffered(1))


def params(mib=60):
    return pltpu.CompilerParams(vmem_limit_bytes=mib * 1024 * 1024)


def far(shape, dtype):
    return pltpu.HBM(shape, dtype)


def from_far(value):
    return pltpu.with_memory_space_constraint(value, pltpu.HBM)


def busy(micros):
    return pl.CostEstimate(flops=int(micros * 1e6), bytes_accessed=0, transcendentals=0)


def row_mean(value):
    return jnp.sum(value, axis=-1, keepdims=True) * (1.0 / D)


def attend_forward(at_ref, own_ref, got_ref, idc_ref, idr_ref, wqkv_ref, bqkv_ref, wo_ref, bo_ref, qkv_ref, xt_ref, ctxt_ref, lse_ref, xhat_ref, inv_ref, x_ref, ctx_ref, mask_ref, stat_ref):
    length = x_ref.shape[0]
    half = length // 2
    x_ref[pl.ds(pl.multiple_of(at_ref[0] * half, half), half), :] = own_ref[...]
    x_ref[pl.ds(pl.multiple_of((1 - at_ref[0]) * half, half), half), :] = got_ref[...]
    xt_ref[...] = jnp.transpose(x_ref[...])
    for c in range(3):
        cols = pl.ds(c * D, D)
        part = mm(x_ref[...], wqkv_ref[:, cols]) + bqkv_ref[:, cols]
        part = part.astype(BF)
        if c == 0:
            part = part * BF(HEAD_DIM**-0.5)
        qkv_ref[:, cols] = part
    mask_ref[...] = jnp.where(idc_ref[...] == idr_ref[...], 0.0, MASK_FILL)
    low = lax.broadcasted_iota(jnp.int32, (length, PAIR), 1) < HEAD_DIM
    low_strip = lax.broadcasted_iota(jnp.int32, (STRIP, PAIR), 1) < HEAD_DIM
    lane = lax.broadcasted_iota(jnp.int32, (STRIP, 128), 1)
    stat_ref[...] = jnp.zeros_like(stat_ref)

    def pair_step(p, carry):
        at = pl.multiple_of(p * PAIR, PAIR)
        keys = qkv_ref[:, pl.ds(D + at, PAIR)]
        values = qkv_ref[:, pl.ds(2 * D + at, PAIR)]
        value_of = [jnp.where(low, values, BF(0)), jnp.where(low, BF(0), values)]
        for s in range(length // STRIP):
            rows = pl.ds(s * STRIP, STRIP)
            queries = qkv_ref[rows, pl.ds(at, PAIR)]
            outs = []
            stats = stat_ref[rows, :]
            for h in range(2):
                query = jnp.where(low_strip, queries, BF(0)) if h == 0 else jnp.where(low_strip, BF(0), queries)
                scores = mm(query, keys, NT) + mask_ref[rows, :]
                top = jnp.max(scores, axis=-1, keepdims=True)
                exps = jnp.exp(scores - top)
                total = jnp.sum(exps, axis=-1, keepdims=True)
                outs.append(mm(exps.astype(BF), value_of[h]) * (1.0 / total))
                stats = jnp.where(lane == 8 * p + h, top + jnp.log(total), stats)
            ctx_ref[rows, pl.ds(at, PAIR)] = (outs[0] + outs[1]).astype(BF)
            stat_ref[rows, :] = stats
        return carry

    lax.fori_loop(0, HEADS // 2, pair_step, 0)
    lse_ref[...] = jnp.transpose(stat_ref[...])[: lse_ref.shape[0], :]
    ctxt_ref[...] = jnp.transpose(ctx_ref[...])
    total_in = mm(ctx_ref[...], wo_ref[...]) + bo_ref[...] + x_ref[...].astype(F32)
    centered = total_in - row_mean(total_in)
    inv = lax.rsqrt(row_mean(centered * centered) + NORM_EPS)
    xhat_ref[...] = centered * inv
    inv_ref[...] = jnp.broadcast_to(inv, inv_ref.shape)


def run_attend_forward(at, hidden, got, ids, wqkv, bqkv, wo, bo):
    rows, half, _ = got.shape
    length = 2 * half
    row_spec = lambda *tail: pl.BlockSpec((None,) + tail, lambda r, at: (r,) + (0,) * len(tail))
    turned = pl.BlockSpec((D, length), lambda r, at: (0, r))
    return pl.pallas_call(
        attend_forward,
        grid_spec=pltpu.PrefetchScalarGridSpec(
            num_scalar_prefetch=1,
            grid=(rows,),
            in_specs=[
                pl.BlockSpec((None, half, D), lambda r, at: (at[0] * rows + r, 0, 0)),
                row_spec(half, D), row_spec(length, 1), row_spec(1, length), whole((D, 3 * D)), whole((1, 3 * D)), whole((D, D)), whole((1, D))],
            out_specs=[row_spec(length, 3 * D), turned, turned, row_spec(STAT_ROWS, length), row_spec(length, D), row_spec(length, 128)],
            scratch_shapes=[pltpu.VMEM((length, D), BF), pltpu.VMEM((length, D), BF), pltpu.VMEM((length, length), F32), pltpu.VMEM((length, 128), F32)],
        ),
        out_shape=[
            far((rows, length, 3 * D), BF),
            far((D, rows * length), BF),
            far((D, rows * length), BF),
            far((rows, STAT_ROWS, length), F32),
            jax.ShapeDtypeStruct((rows, length, D), F32),
            jax.ShapeDtypeStruct((rows, length, 128), F32),
        ],
        compiler_params=params(26),
        cost_estimate=busy(38),
        name="attend_forward",
    )(at, hidden, got, ids[:, :, None], ids[:, None, :], wqkv, bqkv[None], wo, bo[None])


def gelu_parts(value):
    cdf = 0.5 * (1.0 + lax.erf(value * (0.5**0.5)))
    density = jnp.exp(-0.5 * value * value) * 0.3989422804014327
    return cdf, cdf + value * density


def split_terms(value, count):
    parts = []
    for _ in range(count):
        part = value.astype(BF)
        parts.append(part)
        value = value - part.astype(F32)
    return parts


def feed_both(sides_ref, xhat_ref, inv_ref, idc_ref, idr_ref, cnt_ref, pg_ref, ctxt_ref, g1_ref, s1_ref, upb_ref, downb_ref, g2_ref, s2_ref, up_ref, down_ref,
              send_down_ref, keep_down_ref, send_up_ref, keep_up_ref, gh1_ref, gal_ref, pooled_ref, sums1_ref, sums2_ref, ups_ref,
              mid_ref, act_ref, slope_ref, gdl_ref, acc_ref):
    rows, length, _ = xhat_ref.shape
    chunks = FF // D
    half = D // 2
    step = pl.program_id(0)
    core = sides_ref[0]

    @pl.when(step == 0)
    def _():
        for r in range(rows):
            at = pl.ds(r * length, length)
            mid = xhat_ref[r] * g1_ref[...] + s1_ref[...]
            mid_ref[at, :] = mid.astype(BF)
            acc_ref[at, :] = mid + downb_ref[...]

    @pl.when(step < chunks)
    def _():
        cols = pl.ds(pl.multiple_of(step * D, D), D)
        for r in range(rows):
            at = pl.ds(r * length, length)
            pre = mm(mid_ref[at, :], up_ref[...]) + upb_ref[:, cols]
            cdf, slope = gelu_parts(pre)
            act = (pre * cdf).astype(BF)
            act_ref[at, cols] = act
            slope_ref[at, cols] = slope.astype(BF)
            acc_ref[at, :] += mm(act, down_ref[...])

    @pl.when(step == chunks - 1)
    def _():
        def one_row(r, carry):
            at = pl.ds(pl.multiple_of(r * length, length), length)
            total_in = acc_ref[at, :]
            centered = total_in - row_mean(total_in)
            inv = lax.rsqrt(row_mean(centered * centered) + NORM_EPS)
            normed = centered * inv
            final = normed * g2_ref[...] + s2_ref[...]
            member = (lax.broadcasted_iota(jnp.int32, (SEGS, length), 0) == idr_ref[r]).astype(BF)
            pooled_ref[r] = sum(mm(member, part) for part in split_terms(final, 3)) / cnt_ref[r]
            spread = (lax.broadcasted_iota(jnp.int32, (length, SEGS), 1) == idc_ref[r]).astype(BF)
            grad_final = sum(mm(spread, part) for part in split_terms(pg_ref[r] / cnt_ref[r], 3))
            scaled = grad_final * g2_ref[...]
            grad_h2 = inv * (scaled - row_mean(scaled) - normed * row_mean(scaled * normed))
            acc_ref[at, :] = grad_h2
            low = grad_h2.astype(BF)
            gdl_ref[at, :] = low
            sums2_ref[r, 0:1, :] = jnp.sum(grad_final * normed, axis=0, keepdims=True)
            sums2_ref[r, 1:2, :] = jnp.sum(grad_final, axis=0, keepdims=True)
            sums2_ref[r, 2:3, :] = jnp.sum(low.astype(F32), axis=0, keepdims=True)
            return carry

        lax.fori_loop(0, rows, one_row, 0)

    away = pl.ds(pl.multiple_of((1 - core) * half, half), half)
    here = pl.ds(pl.multiple_of(core * half, half), half)

    @pl.when((step >= chunks) & (step < 2 * chunks))
    def _():
        chunk = chunk_of(step, core, chunks)
        cols = pl.ds(pl.multiple_of(chunk * D, D), D)
        total = jnp.zeros((1, D), F32)
        for r in range(rows):
            at = pl.ds(r * length, length)
            grad_act = mm(gdl_ref[at, :], down_ref[...], NT)
            low = (grad_act * slope_ref[at, cols].astype(F32)).astype(BF)
            slope_ref[at, cols] = low
            total += jnp.sum(low.astype(F32), axis=0, keepdims=True)
            acc_ref[at, :] += mm(low, up_ref[...], NT)
        ups_ref[:, cols] = total
        low = slope_ref[:, cols]
        send_up_ref[...] = mm(mid_ref[:, away], low, TN).astype(BF)
        keep_up_ref[...] = mm(mid_ref[:, here], low, TN).astype(BF)

    for first, out in ((chunks, send_down_ref), (chunks + chunks // 2, keep_down_ref)):

        @pl.when((step >= first) & (step < first + chunks // 2))
        def _(out=out):
            cols = pl.ds(pl.multiple_of(chunk_of(step, core, chunks) * D, D), D)
            out[...] = mm(act_ref[:, cols], gdl_ref[...], TN).astype(BF)

    @pl.when(step == 2 * chunks)
    def _():
        def one_row(r, carry):
            at = pl.ds(pl.multiple_of(r * length, length), length)
            grad_mid = acc_ref[at, :]
            normed = xhat_ref[r]
            scaled = grad_mid * g1_ref[...]
            grad_h1 = inv_ref[r, :, 0:1] * (scaled - row_mean(scaled) - normed * row_mean(scaled * normed))
            gh1_ref[r] = grad_h1
            low = grad_h1.astype(BF)
            gal_ref[r] = low
            gdl_ref[at, :] = low
            sums1_ref[r, 0:1, :] = jnp.sum(grad_mid * normed, axis=0, keepdims=True)
            sums1_ref[r, 1:2, :] = jnp.sum(grad_mid, axis=0, keepdims=True)
            sums1_ref[r, 2:3, :] = jnp.sum(low.astype(F32), axis=0, keepdims=True)
            return carry

        lax.fori_loop(0, rows, one_row, 0)
        send_up_ref[...] = mm(ctxt_ref[away, :], gdl_ref[...]).astype(BF)
        keep_up_ref[...] = mm(ctxt_ref[here, :], gdl_ref[...]).astype(BF)


def chunk_of(step, core, chunks):
    back = step - chunks
    half = chunks // 2
    later = back - half
    return jnp.where(step < chunks, step, jnp.where(back < half, (1 - core) * half + back, core * half + jnp.minimum(later, half - 1)))


def run_feed_both(sides, xhat, inv, ids, counts, pooled_grad, ctxt, g1, s1, up, upb, down, downb, g2, s2):
    rows, length, _ = xhat.shape
    tokens, chunks, half = rows * length, FF // D, D // 2
    halves = chunks // 2
    vectors = [g1[None], s1[None], upb[None], downb[None], g2[None], s2[None]]
    counts = counts.astype(F32)[:, :, None]
    ready = [xhat, inv, ids[:, :, None], ids[:, None, :], counts, pooled_grad, from_far(ctxt), *vectors]
    fixed = lambda shape: pl.BlockSpec(shape, lambda t, sd: (0,) * len(shape), pipeline_mode=pl.Buffered(1))
    backward = lambda t, sd: chunk_of(jnp.maximum(t, chunks), sd[0], chunks)
    up_at = lambda t, sd: (0, jnp.where(t < 2 * chunks, backward(t, sd), chunks))
    return pl.pallas_call(
        feed_both,
        grid_spec=pltpu.PrefetchScalarGridSpec(
            num_scalar_prefetch=1,
            grid=(2 * chunks + 1,),
            in_specs=[fixed(v.shape) for v in ready]
            + [pl.BlockSpec((D, D), lambda t, sd: (0, chunk_of(t, sd[0], chunks))), pl.BlockSpec((D, D), lambda t, sd: (chunk_of(t, sd[0], chunks), 0))],
            out_specs=[
                pl.BlockSpec((D, D), lambda t, sd: (jnp.clip(t - chunks, 0, halves - 1), 0)),
                pl.BlockSpec((D, D), lambda t, sd: (jnp.clip(t - chunks - halves, 0, halves - 1), 0)),
                pl.BlockSpec((half, D), up_at),
                pl.BlockSpec((half, D), up_at),
                fixed((rows, length, D)),
                fixed((rows, length, D)),
                fixed((rows, SEGS, D)),
                fixed((rows, 8, D)),
                fixed((rows, 8, D)),
                fixed((1, FF)),
            ],
            scratch_shapes=[
                pltpu.VMEM((tokens, D), BF),
                pltpu.VMEM((tokens, FF), BF),
                pltpu.VMEM((tokens, FF), BF),
                pltpu.VMEM((tokens, D), BF),
                pltpu.VMEM((tokens, D), F32),
            ],
        ),
        out_shape=[
            far((FF // 2, D), BF),
            far((FF // 2, D), BF),
            far((half, FF + D), BF),
            far((half, FF + D), BF),
            far((rows, length, D), F32),
            far((rows, length, D), BF),
            jax.ShapeDtypeStruct((rows, SEGS, D), F32),
            jax.ShapeDtypeStruct((rows, 8, D), F32),
            jax.ShapeDtypeStruct((rows, 8, D), F32),
            jax.ShapeDtypeStruct((1, FF), F32),
        ],
        compiler_params=params(52),
        cost_estimate=busy(50),
        name="feed_both",
    )(sides, *ready, from_far(up), from_far(down))


GROUP = 2
GROUP_WIDTH = GROUP * PAIR


def attend_backward(gal_ref, q_ref, k_ref, v_ref, lse_ref, idc_ref, idr_ref, wo_ref, gqkv_ref, sums_ref, mask_ref, gctx_ref):
    length = gal_ref.shape[0]
    gctx_ref[...] = mm(gal_ref[...], wo_ref[...], NT).astype(BF)
    mask_ref[...] = jnp.where(idc_ref[...] == idr_ref[...], 0.0, MASK_FILL)
    low_strip = lax.broadcasted_iota(jnp.int32, (STRIP, PAIR), 1) < HEAD_DIM
    low = lax.broadcasted_iota(jnp.int32, (length, PAIR), 1) < HEAD_DIM

    def pair_step(p, carry):
        at = pl.multiple_of(p * PAIR, PAIR)
        keys = k_ref[:, pl.ds(at, PAIR)]
        values = v_ref[:, pl.ds(at, PAIR)]
        key_of = [jnp.where(low, keys, BF(0)), jnp.where(low, BF(0), keys)]
        grad_k = jnp.zeros((length, PAIR), F32)
        grad_v = jnp.zeros((length, PAIR), F32)
        for s in range(length // STRIP):
            rows = pl.ds(s * STRIP, STRIP)
            lses = lse_ref[pl.ds(pl.multiple_of(8 * p, 8), 8), rows]
            queries = q_ref[rows, pl.ds(at, PAIR)]
            grads = gctx_ref[rows, pl.ds(at, PAIR)]
            grad_q = jnp.zeros((STRIP, PAIR), F32)
            for h in range(2):
                pick = (lambda v: jnp.where(low_strip, v, BF(0))) if h == 0 else (lambda v: jnp.where(low_strip, BF(0), v))
                query, grad = pick(queries), pick(grads)
                scores = mm(keys, query, NT) + mask_ref[:, rows]
                probs = jnp.exp(scores - lses[h : h + 1, :])
                grad_p = mm(values, grad, NT)
                inner = jnp.sum(probs * grad_p, axis=0, keepdims=True)
                grad_s = (probs * (grad_p - inner)).astype(BF)
                grad_v += mm(probs.astype(BF), grad)
                grad_k += mm(grad_s, query)
                grad_q += mm(grad_s, key_of[h], TN)
            gqkv_ref[rows, pl.ds(at, PAIR)] = (grad_q * HEAD_DIM**-0.5).astype(BF)
        gqkv_ref[:, pl.ds(GROUP_WIDTH + at, PAIR)] = grad_k.astype(BF)
        gqkv_ref[:, pl.ds(2 * GROUP_WIDTH + at, PAIR)] = grad_v.astype(BF)
        return carry

    lax.fori_loop(0, GROUP, pair_step, 0)
    sums_ref[...] = jnp.sum(gqkv_ref[...].astype(F32), axis=0, keepdims=True)


def run_attend_backward(group, gal, qkv, lse, ids, wo):
    rows, length, _ = gal.shape
    groups = D // GROUP_WIDTH
    row_spec = lambda *tail: pl.BlockSpec((None,) + tail, lambda r: (r,) + (0,) * len(tail))
    part = lambda c: pl.BlockSpec((None, length, GROUP_WIDTH), lambda r: (r, 0, c * groups + group))
    return pl.pallas_call(
        attend_backward,
        grid=(rows,),
        in_specs=[
            row_spec(length, D), part(0), part(1), part(2),
            pl.BlockSpec((None, 8 * GROUP, length), lambda r: (r, group, 0)),
            row_spec(length, 1), row_spec(1, length),
            pl.BlockSpec((GROUP_WIDTH, D), lambda r: (group, 0)),
        ],
        out_specs=[row_spec(length, 3 * GROUP_WIDTH), row_spec(1, 3 * GROUP_WIDTH)],
        scratch_shapes=[pltpu.VMEM((length, length), F32), pltpu.VMEM((length, GROUP_WIDTH), BF)],
        out_shape=[far((rows, length, 3 * GROUP_WIDTH), BF), jax.ShapeDtypeStruct((rows, 1, 3 * GROUP_WIDTH), F32)],
        compiler_params=params(20),
        cost_estimate=busy(14),
        name="attend_backward",
    )(from_far(gal), *[from_far(qkv)] * 3, from_far(lse), ids[:, :, None], ids[:, None, :], from_far(wo))


def input_grad(at_ref, gh1_ref, *refs):
    parts, (wqkv_ref, own_ref, send_ref) = refs[:-3], refs[-3:]
    half = gh1_ref.shape[0] // 2
    for out, first in ((own_ref, at_ref[0]), (send_ref, 1 - at_ref[0])):
        rows = pl.ds(pl.multiple_of(first * half, half), half)
        total = gh1_ref[rows, :]
        for g, part in enumerate(parts):
            for c in range(3):
                total += mm(part[rows, c * GROUP_WIDTH : (c + 1) * GROUP_WIDTH], wqkv_ref[:, c * D + g * GROUP_WIDTH : c * D + (g + 1) * GROUP_WIDTH], NT)
        out[...] = total.astype(BF)


def run_input_grad(at, gh1, parts, wqkv):
    rows, length, _ = gh1.shape
    half = length // 2
    row_spec = lambda *tail: pl.BlockSpec((None,) + tail, lambda r, at: (r,) + (0,) * len(tail))
    return pl.pallas_call(
        input_grad,
        grid_spec=pltpu.PrefetchScalarGridSpec(
            num_scalar_prefetch=1,
            grid=(rows,),
            in_specs=[row_spec(length, D)] + [row_spec(length, 3 * GROUP_WIDTH)] * len(parts) + [whole((D, 3 * D))],
            out_specs=[row_spec(half, D), row_spec(half, D)],
        ),
        out_shape=[jax.ShapeDtypeStruct((rows, half, D), BF)] * 2,
        compiler_params=params(18),
        cost_estimate=busy(6),
        name="input_grad",
    )(at, from_far(gh1), *map(from_far, parts), from_far(wqkv))


SMALLS = 128


def gather_small(sums1_ref, sums2_ref, ups_ref, sq_refs, small_ref, pack_ref):
    pack_ref[...] = jnp.zeros_like(pack_ref)
    total = lambda ref: jnp.sum(ref[...], axis=0)
    first, second, ups = total(sums1_ref), total(sums2_ref), ups_ref[...]
    for g, ref in enumerate(sq_refs):
        cols = slice(g * GROUP_WIDTH, (g + 1) * GROUP_WIDTH)
        pack_ref[0:1, cols] = total(ref)[:, :GROUP_WIDTH]
        pack_ref[1:2, cols] = total(ref)[:, 2 * GROUP_WIDTH :]
    lines = [first[2:3], first[0:1], first[1:2], second[2:3], second[0:1], second[1:2]]
    lines += [ups[:, i * D : (i + 1) * D] for i in range(FF // D)]
    for i, line in enumerate(lines):
        pack_ref[i + 2 : i + 3, :] = line
    small_ref[...] = jnp.transpose(pack_ref[...])


def qkv_grads_body(parts, sides_ref, x_away_ref, x_here_ref, *refs):
    grads, refs = refs[:parts], refs[parts:]
    small_in, (away_ref, here_ref, small_ref, pack_ref) = refs[:-4], refs[-4:]
    half, wide = x_away_ref.shape[0], 3 * GROUP_WIDTH
    gather_small(*small_in[:3], small_in[3:], small_ref, pack_ref)
    for left, out, first in ((x_away_ref, away_ref, 1 - sides_ref[0]), (x_here_ref, here_ref, sides_ref[0])):
        for g, grad in enumerate(grads):
            out[:, g * wide : (g + 1) * wide] = mm(left[...], grad[...]).astype(BF)
        rows = pl.ds(pl.multiple_of(first * half, half), half)
        out[:, parts * wide :] = small_ref[rows, :].astype(BF)


def qkv_grads(sides, x, grads, smalls):
    half, tokens = D // 2, x.shape[1]
    width = 3 * GROUP_WIDTH * len(grads) + SMALLS
    return pl.pallas_call(
        functools.partial(qkv_grads_body, len(grads)),
        grid_spec=pltpu.PrefetchScalarGridSpec(
            num_scalar_prefetch=1,
            grid=(1,),
            in_specs=[pl.BlockSpec((half, tokens), lambda j, sd: (1 - sd[0], 0)), pl.BlockSpec((half, tokens), lambda j, sd: (sd[0], 0))]
            + [whole(v.shape) for v in (*grads, *smalls)],
            out_specs=[pl.BlockSpec((half, width), lambda j, sd: (0, 0))] * 2,
            scratch_shapes=[pltpu.VMEM((D, SMALLS), F32), pltpu.VMEM((SMALLS, D), F32)],
        ),
        out_shape=[far((half, width), BF)] * 2,
        compiler_params=params(24),
        cost_estimate=busy(7),
        name="qkv_grads",
    )(sides, *[from_far(x)] * 2, *map(from_far, grads), *smalls)


def add_split_body(at_ref, keep_away_ref, keep_here_ref, got_away_ref, got_here_ref, send_ref, next_ref):
    send_ref[...] = (keep_away_ref[...].astype(F32) + got_away_ref[...].astype(F32)).astype(BF)
    next_ref[...] = keep_here_ref[...].astype(F32) + got_here_ref[...].astype(F32)


def add_split(at, keep, got):
    half, width = keep.shape[0] // 2, keep.shape[1]
    cols = width // 2 if width % 256 == 0 else width
    away = pl.BlockSpec((half, cols), lambda j, at: (1 - at[0], j))
    here = pl.BlockSpec((half, cols), lambda j, at: (at[0], j))
    return pl.pallas_call(
        add_split_body,
        grid_spec=pltpu.PrefetchScalarGridSpec(
            num_scalar_prefetch=1,
            grid=(width // cols,),
            in_specs=[away, here, away, here],
            out_specs=[pl.BlockSpec((half, cols), lambda j, at: (0, j))] * 2,
        ),
        out_shape=[far((half, width), BF), far((half, width), F32)],
        compiler_params=params(16),
        cost_estimate=busy(3),
        name="add_split",
    )(at, *[from_far(keep)] * 2, got, got)


def assemble_body(steps, moves, place_ref, *refs):
    outs = refs[len(refs) - len(moves) :]
    pieces = refs[: len(refs) - len(moves)]
    at = pl.program_id(0) // steps
    for p in range(4):

        @pl.when(at == p)
        def _(p=p):
            for out, parts in zip(outs, moves):
                for source, first, width, to in parts:
                    out[:, to : to + width] = pieces[4 * source + p][:, first : first + width].astype(F32)


def assemble(places, sources, moves):
    quarter = sources[0][0].shape[0]
    block = min(quarter, 384)
    steps = quarter // block
    widths = [sum(part[2] for part in parts) for parts in moves]
    piece_at = lambda p, width: pl.BlockSpec((block, width), lambda i, pos: (jnp.clip(i - p * steps, 0, steps - 1), 0))
    return pl.pallas_call(
        functools.partial(assemble_body, steps, moves),
        grid_spec=pltpu.PrefetchScalarGridSpec(
            num_scalar_prefetch=1,
            grid=(4 * steps,),
            in_specs=[piece_at(p, pieces[p].shape[1]) for pieces in sources for p in range(4)],
            out_specs=[pl.BlockSpec((block, w), lambda i, pos: (pos[i // steps] * steps + i % steps, 0)) for w in widths],
        ),
        out_shape=[jax.ShapeDtypeStruct((4 * quarter, w), F32) for w in widths],
        compiler_params=params(36),
        cost_estimate=busy(8),
        name="assemble",
    )(places, *[piece for pieces in sources for piece in pieces])


class Links:
    def __init__(self):
        dp, seq = lax.axis_size("dp"), lax.axis_size("seq")
        dp_at, seq_at = lax.axis_index("dp"), lax.axis_index("seq")
        self.core = dp_at % 2

        def flip(bit_of):
            pairs = []
            for d in range(dp):
                for s in range(seq):
                    bit = bit_of(d % 2)
                    to = (d, s ^ 1) if bit < 0 else (d ^ (1 << bit), s)
                    pairs.append((d * seq + s, to[0] * seq + to[1]))
            return pairs

        second = (dp_at >> 1) % 2
        self.side_a = jnp.where(self.core == 0, second, seq_at)
        self.side_b = jnp.where(self.core == 0, seq_at, second)
        self.pairs_core = flip(lambda c: 0)
        self.pairs_a = flip(lambda c: 1 if c == 0 else -1)
        self.pairs_b = flip(lambda c: -1 if c == 0 else 1)
        bits = list(range(2, (dp - 1).bit_length()))
        self.rest = []
        for first in range(0, len(bits), 2):
            part = bits[first : first + 2]
            size = 1 << len(part)
            routes = [[(d * seq + s, (d ^ (hop << part[0])) * seq + s) for d in range(dp) for s in range(seq)] for hop in range(1, size)]
            self.rest.append((routes, (dp_at >> part[0]) % size))
        self.sides = jnp.stack([self.core, self.side_a]).astype(jnp.int32)
        self.side_a_array = self.side_a.astype(jnp.int32).reshape(1)
        self.side_b_array = self.side_b.astype(jnp.int32).reshape(1)
        other = 2 * (1 - self.core)
        mine = 2 * self.core
        self.places = jnp.stack([mine + self.side_a, mine + 1 - self.side_a, other + self.side_b, other + 1 - self.side_b]).astype(jnp.int32)

    def send(self, value, pairs):
        return lax.ppermute(value, ("dp", "seq"), pairs)


class Order:
    def __init__(self):
        self.last = None

    def run(self, step, first, *others):
        if self.last is not None:
            first, self.last = lax.optimization_barrier((first, self.last))
        out = step(first, *others)
        self.last = jax.tree.leaves(out)[0]
        return out

    def arrive(self, value):
        value, self.last = lax.optimization_barrier((value, self.last))
        return value


def collect(at, pieces):
    swap = 1
    while swap < len(pieces):
        bit = (at // swap) % 2
        pieces = [jnp.where(bit == 0, pieces[i], pieces[i ^ swap]) for i in range(len(pieces))]
        swap *= 2
    return jnp.concatenate(pieces)


def exchange(order, links, away, keep, done, finish):
    got = links.send(away, links.pairs_core)
    yield
    away, keep = order.run(lambda g: add_split(links.side_a_array, keep, g), got)
    got = links.send(away, links.pairs_a)
    yield
    away, keep = order.run(lambda g: add_split(links.side_b_array, keep, g), got)
    got = links.send(away, links.pairs_b)
    yield
    for routes, at in links.rest:
        piece = keep.shape[0] // (len(routes) + 1)

        def deal(got, keep=keep, at=at, piece=piece, routes=routes):
            part = lambda v, to: lax.dynamic_slice_in_dim(v, to * piece, piece, 0).astype(F32)
            both = lambda to: part(keep, to) + part(got, to)
            return [both(at ^ hop).astype(BF) for hop in range(1, len(routes) + 1)], both(at)

        parts, keep = order.run(deal, got)
        got = [links.send(p, pairs) for p, pairs in zip(parts, routes)]
        yield
        got = order.run(lambda g, *rest: sum(v.astype(F32) for v in (g, *rest)), *got)
    cur = (keep + got.astype(F32)).astype(BF)
    for routes, at in links.rest[::-1]:
        got = [links.send(cur, pairs) for pairs in routes]
        yield
        cur = order.run(lambda g, *rest: collect(at, [cur, g, *rest]), *got)
    got = links.send(cur, links.pairs_b)
    yield
    cur = order.run(lambda g: collect(links.side_b, [cur, g]), got)
    got = links.send(cur, links.pairs_a)
    across = links.send(cur, links.pairs_core)
    yield
    got = order.arrive(got)
    done.append([cur, got, across, links.send(got, links.pairs_core)])
    yield
    if finish is not None:
        done.append(order.run(lambda g: finish([cur, got, across, g]), done[0][3]))
        yield


SCHEDULE = "mduqmmqqdmudqumdqudmqumdquqddqududduquudu"


def swap_seq(value):
    return lax.ppermute(value, "seq", [(0, 1), (1, 0)])


def local(
    hidden_in,
    segment_ids,
    segment_counts,
    pooled_grad,
    qkv_weight,
    query_bias,
    value_bias,
    out_weight,
    out_bias,
    norm1_gain,
    norm1_shift,
    up_weight,
    up_bias,
    down_weight,
    down_bias,
    norm2_gain,
    norm2_shift,
):
    links = Links()
    seq_at = lax.axis_index("seq")
    seq_array = seq_at.astype(jnp.int32).reshape(1)
    micro, row_count, piece, _ = hidden_in.shape
    length = piece * 2
    own_micro = micro // 2
    rows = own_micro * row_count
    tokens = rows * length

    def own_part(value):
        return lax.dynamic_slice_in_dim(value, seq_at * own_micro, own_micro, 0)

    got = swap_seq(lax.dynamic_slice_in_dim(hidden_in, (1 - seq_at) * own_micro, own_micro, 0))
    counts = own_part(segment_counts).reshape(rows, SEGS)
    pooled_cot = own_part(pooled_grad).reshape(rows, SEGS, D)
    seg = jnp.arange(SEGS, dtype=jnp.int32)
    ends = jnp.sum(jnp.where(seg[None, :, None] <= seg[None, None, :], counts[:, :, None], 0), axis=1)
    positions = jnp.arange(length, dtype=jnp.int32)
    ids = jnp.sum((positions[None, :, None] >= ends[:, None, :-1]).astype(jnp.int32), axis=-1)
    shift_qkv = jnp.concatenate([query_bias, jnp.zeros((D,), F32), value_bias])

    order = Order()
    qkv, x_turned, ctx_turned, lse, xhat, inv = run_attend_forward(
        seq_array,
        hidden_in.reshape(micro * row_count, piece, D),
        got.reshape(rows, piece, D),
        ids,
        qkv_weight,
        shift_qkv,
        out_weight,
        out_bias,
    )
    order.last = xhat
    away_down, keep_down, away_up, keep_up, grad_h1, grad_attn_low, pooled, sums1, sums2, ups = run_feed_both(
        links.sides, xhat, inv, ids, counts, pooled_cot, ctx_turned, norm1_gain, norm1_shift,
        up_weight, up_bias, down_weight, down_bias, norm2_gain, norm2_shift,
    )
    order.last = away_down
    streams, sums, state = {}, {name: [] for name in ("down", "up", "qkv")}, {}
    finishes = {
        "down": lambda pieces: assemble(links.places, [pieces], [[(0, 0, D, 0)]]),
        "up": lambda pieces: assemble(links.places, [pieces], [[(0, 0, FF, 0)], [(0, FF, D, 0)]]),
    }

    def start(name, away, keep):
        streams[name] = exchange(order, links, away, keep, sums[name], finishes.get(name))
        next(streams[name])

    def joined(first, second):
        return jnp.where(seq_at == 0, jnp.concatenate([first, second]), jnp.concatenate([second, first]))

    def main_steps():
        start("down", away_down, keep_down)
        start("up", away_up, keep_up)
        pooled_own = pooled.reshape(own_micro, row_count, SEGS, D)
        pooled_got = swap_seq(pooled_own)
        grads, sums_qkv = [], []
        for group in range(D // GROUP_WIDTH):
            grad, total = order.run(lambda g: run_attend_backward(group, g, qkv, lse, ids, out_weight), grad_attn_low)
            grads.append(grad)
            sums_qkv.append(total)
            yield
        flat = [g.reshape(tokens, 3 * GROUP_WIDTH) for g in grads]
        smalls = (sums1, sums2, ups, *sums_qkv)
        start("qkv", *order.run(lambda g: qkv_grads(links.sides, x_turned, [*flat[:-1], g], smalls), flat[-1]))
        yield
        back_own, back_send = order.run(lambda g: run_input_grad(seq_array, g, grads, qkv_weight), grad_h1)
        shape = (own_micro, row_count, piece, D)
        back_own, back_got = back_own.reshape(shape), swap_seq(back_send.reshape(shape))
        yield
        state["pooled"] = order.run(lambda g: joined(pooled_own, g), pooled_got)
        yield
        state["input"] = order.run(lambda g: joined(back_own, g), back_got)
        yield

    streams["main"] = main_steps()
    for name in map({"m": "main", "d": "down", "u": "up", "q": "qkv"}.get, SCHEDULE):
        if name in streams:
            next(streams[name], None)
    while streams:
        for name in list(streams):
            if next(streams[name], streams) is streams:
                del streams[name]
    pooled_local, input_local = state["pooled"], state["input"]
    (down_all,) = sums["down"][1]
    up_all, out_all = sums["up"][1]
    wide = 3 * GROUP_WIDTH
    columns = [(0, g * wide + c * GROUP_WIDTH, GROUP_WIDTH, c * D + g * GROUP_WIDTH) for g in range(D // GROUP_WIDTH) for c in range(3)]
    qkv_all, small_all = assemble(links.places, sums["qkv"], [columns, [(0, 3 * D, SMALLS, 0)]])
    lines = small_all[:, : 8 + FF // D].T
    return (
        pooled_local,
        input_local,
        qkv_all,
        lines[0],
        lines[1],
        out_all,
        lines[2],
        lines[3],
        lines[4],
        up_all,
        lines[8 : 8 + FF // D].reshape(FF),
        down_all,
        lines[5],
        lines[6],
        lines[7],
    )


def solution(mesh):
    rep = P()
    in_specs = (
        P(None, "dp", "seq", None),
        P(None, "dp", "seq"),
        P(None, "dp", None),
        P(None, "dp", None, None),
    ) + (rep,) * 13
    out_specs = (P(None, "dp", None, None), P(None, "dp", "seq", None)) + (rep,) * 13
    return jax.shard_map(local, mesh=mesh, in_specs=in_specs, out_specs=out_specs, check_vma=False)
```

```python
import functools

import jax
import jax.numpy as jnp
from jax import lax
from jax.experimental import pallas as pl
from jax.experimental.pallas import tpu as pltpu
from jax.sharding import PartitionSpec as P

D = 768
HEADS = 12
HEAD_DIM = 64
FF = 3072
SEGS = 32
NORM_EPS = 1e-05
MASK_FILL = -1e30
BF = jnp.bfloat16
F32 = jnp.float32
PAIR = 2 * HEAD_DIM
STRIP = 512
CHUNK = 1024
STAT_ROWS = 4 * HEADS

NN = (((1,), (0,)), ((), ()))
NT = (((1,), (1,)), ((), ()))
TN = (((0,), (0,)), ((), ()))


def mm(left, right, dims=NN):
    return lax.dot_general(left, right, dims, preferred_element_type=F32)


def whole(shape):
    zeros = (0,) * len(shape)
    return pl.BlockSpec(shape, lambda *_: zeros, pipeline_mode=pl.Buffered(1))


def params(mib=60):
    return pltpu.CompilerParams(vmem_limit_bytes=mib * 1024 * 1024)


def far(shape, dtype):
    return pltpu.HBM(shape, dtype)


def from_far(value):
    return pltpu.with_memory_space_constraint(value, pltpu.HBM)


def busy(micros):
    return pl.CostEstimate(flops=int(micros * 2e8), bytes_accessed=0, transcendentals=0)


def membership(counts, length):
    here = lax.broadcasted_iota(jnp.int32, (SEGS, SEGS), 0)
    other = lax.broadcasted_iota(jnp.int32, (SEGS, SEGS), 1)
    spread = jnp.broadcast_to(counts, (SEGS, SEGS))
    ends = jnp.sum(jnp.where(other <= here, spread, 0), axis=1, keepdims=True)
    sizes = jnp.sum(jnp.where(other == here, spread, 0), axis=1, keepdims=True)
    at = lax.broadcasted_iota(jnp.int32, (SEGS, length), 1)
    return ((at < ends) & (at >= ends - sizes)).astype(F32).astype(BF), sizes.astype(F32)


def fill_mask(mask_ref, counts):
    member, _ = membership(counts, mask_ref.shape[0])
    mask_ref[...] = jnp.where(mm(member, member, TN) > 0.5, 0.0, MASK_FILL)


def row_mean(value):
    return jnp.sum(value, axis=-1, keepdims=True) * (1.0 / D)


def attend_forward(at_ref, own_ref, got_ref, cnt_ref, wqkv_ref, bq_ref, bv_ref, wo_ref, bo_ref, *refs):
    qkv_ref, xt_ref, ctxt_ref, lse_ref, xhat_ref, inv_ref, x_ref, ctx_ref, mask_ref, stat_ref = refs[-10:]
    length = x_ref.shape[0]
    half = length // 2
    x_ref[pl.ds(pl.multiple_of(at_ref[0] * half, half), half), :] = own_ref[...]
    x_ref[pl.ds(pl.multiple_of((1 - at_ref[0]) * half, half), half), :] = got_ref[...]
    xt_ref[...] = jnp.transpose(x_ref[...])
    for c in range(3):
        cols = pl.ds(c * D, D)
        part = mm(x_ref[...], wqkv_ref[:, cols])
        if c == 0:
            part = (part + bq_ref[...]).astype(BF) * BF(HEAD_DIM**-0.5)
        elif c == 2:
            part = part + bv_ref[...]
        qkv_ref[:, cols] = part.astype(BF)
    fill_mask(mask_ref, cnt_ref[...])
    low = lax.broadcasted_iota(jnp.int32, (length, PAIR), 1) < HEAD_DIM
    low_strip = lax.broadcasted_iota(jnp.int32, (STRIP, PAIR), 1) < HEAD_DIM
    lane = lax.broadcasted_iota(jnp.int32, (STRIP, 128), 1)
    stat_ref[...] = jnp.zeros_like(stat_ref)

    def pair_step(p, carry):
        at = pl.multiple_of(p * PAIR, PAIR)
        keys = qkv_ref[:, pl.ds(D + at, PAIR)]
        values = qkv_ref[:, pl.ds(2 * D + at, PAIR)]
        value_of = [jnp.where(low, values, BF(0)), jnp.where(low, BF(0), values)]
        for s in range(length // STRIP):
            rows = pl.ds(s * STRIP, STRIP)
            queries = qkv_ref[rows, pl.ds(at, PAIR)]
            outs = []
            stats = stat_ref[rows, :]
            for h in range(2):
                query = jnp.where(low_strip, queries, BF(0)) if h == 0 else jnp.where(low_strip, BF(0), queries)
                scores = mm(query, keys, NT) + mask_ref[rows, :]
                top = jnp.max(scores, axis=-1, keepdims=True)
                exps = jnp.exp(scores - top)
                total = jnp.sum(exps, axis=-1, keepdims=True)
                outs.append(mm(exps.astype(BF), value_of[h]) * (1.0 / total))
                stats = jnp.where(lane == 8 * p + h, top + jnp.log(total), stats)
            ctx_ref[rows, pl.ds(at, PAIR)] = (outs[0] + outs[1]).astype(BF)
            stat_ref[rows, :] = stats
        return carry

    lax.fori_loop(0, HEADS // 2, pair_step, 0, unroll=2)
    lse_ref[...] = jnp.transpose(stat_ref[...])[: lse_ref.shape[0], :]
    ctxt_ref[...] = jnp.transpose(ctx_ref[...])
    total_in = mm(ctx_ref[...], wo_ref[...]) + bo_ref[...] + x_ref[...].astype(F32)
    centered = total_in - row_mean(total_in)
    inv = lax.rsqrt(row_mean(centered * centered) + NORM_EPS)
    xhat_ref[...] = centered * inv
    inv_ref[...] = jnp.broadcast_to(inv, inv_ref.shape)


def run_attend_forward(row, rows, at, hidden, got, counts, wqkv, bq, bv, wo, bo, before):
    half = got.shape[0]
    length = 2 * half
    row_spec = lambda *tail: pl.BlockSpec((None,) + tail, lambda r, at: (row,) + (0,) * len(tail))
    turned = pl.BlockSpec((D, length), lambda r, at: (0, row))
    return pl.pallas_call(
        attend_forward,
        grid_spec=pltpu.PrefetchScalarGridSpec(
            num_scalar_prefetch=1,
            grid=(1,),
            in_specs=[
                pl.BlockSpec((None, half, D), lambda r, at: (at[0] * rows + row, 0, 0)),
                whole((half, D)), pl.BlockSpec((None, 1, SEGS), lambda r, at: (at[0] * rows + row, 0, 0)), whole((D, 3 * D)), whole((1, D)), whole((1, D)), whole((D, D)), whole((1, D))]
            + [pl.BlockSpec(memory_space=pl.ANY)] * len(before),
            out_specs=[row_spec(length, 3 * D), turned, turned, row_spec(STAT_ROWS, length), row_spec(length, D), row_spec(length, 128)],
            scratch_shapes=[pltpu.VMEM((length, D), BF), pltpu.VMEM((length, D), BF), pltpu.VMEM((length, length), F32), pltpu.VMEM((length, 128), F32)],
        ),
        out_shape=[
            jax.ShapeDtypeStruct((rows, length, 3 * D), BF),
            far((D, rows * length), BF),
            far((D, rows * length), BF),
            jax.ShapeDtypeStruct((rows, STAT_ROWS, length), F32),
            jax.ShapeDtypeStruct((rows, length, D), F32),
            jax.ShapeDtypeStruct((rows, length, 128), F32),
        ],
        input_output_aliases={9 + i: i for i in range(len(before))},
        compiler_params=params(26),
        cost_estimate=busy(38),
        name="attend_forward",
    )(at, hidden, got, counts, from_far(wqkv), bq[None], bv[None], from_far(wo), bo[None], *before)


def gelu_parts(value):
    cdf = 0.5 * (1.0 + lax.erf(value * (0.5**0.5)))
    density = jnp.exp(-0.5 * value * value) * 0.3989422804014327
    return cdf, cdf + value * density


def split_terms(value, count):
    parts = []
    for _ in range(count):
        part = value.astype(BF)
        parts.append(part)
        value = value - part.astype(F32)
    return parts


def feed_both(sides_ref, xhat_ref, inv_ref, cnt_ref, pg_ref, ctxt_ref, g1_ref, s1_ref, upb_ref, downb_ref, g2_ref, s2_ref, up_ref, down_ref,
              send_down_ref, keep_down_ref, send_up_ref, keep_up_ref, gh1_ref, gal_ref, pooled_ref, sums1_ref, sums2_ref, ups_ref,
              mid_ref, act_ref, slope_ref, gdl_ref, acc_ref):
    rows, length, _ = xhat_ref.shape
    chunks = FF // D
    half = D // 2
    step = pl.program_id(0)
    core = sides_ref[0]

    @pl.when(step == 0)
    def _():
        for r in range(rows):
            at = pl.ds(r * length, length)
            mid = xhat_ref[r] * g1_ref[...] + s1_ref[...]
            mid_ref[at, :] = mid.astype(BF)
            acc_ref[at, :] = mid + downb_ref[...]

    @pl.when(step < chunks)
    def _():
        cols = pl.ds(pl.multiple_of(step * D, D), D)
        for r in range(rows):
            at = pl.ds(r * length, length)
            pre = mm(mid_ref[at, :], up_ref[...]) + upb_ref[:, cols]
            cdf, slope = gelu_parts(pre)
            act = (pre * cdf).astype(BF)
            act_ref[at, cols] = act
            slope_ref[at, cols] = slope.astype(BF)
            acc_ref[at, :] += mm(act, down_ref[...])

    @pl.when(step == chunks - 1)
    def _():
        def one_row(r, carry):
            at = pl.ds(pl.multiple_of(r * length, length), length)
            total_in = acc_ref[at, :]
            centered = total_in - row_mean(total_in)
            inv = lax.rsqrt(row_mean(centered * centered) + NORM_EPS)
            normed = centered * inv
            final = normed * g2_ref[...] + s2_ref[...]
            member, sizes = membership(cnt_ref[r], length)
            pooled_ref[r] = sum(mm(member, part) for part in split_terms(final, 3)) / sizes
            grad_final = sum(mm(member, part, TN) for part in split_terms(pg_ref[r] / sizes, 3))
            scaled = grad_final * g2_ref[...]
            grad_h2 = inv * (scaled - row_mean(scaled) - normed * row_mean(scaled * normed))
            acc_ref[at, :] = grad_h2
            low = grad_h2.astype(BF)
            gdl_ref[at, :] = low
            sums2_ref[r, 0:1, :] = jnp.sum(grad_final * normed, axis=0, keepdims=True)
            sums2_ref[r, 1:2, :] = jnp.sum(grad_final, axis=0, keepdims=True)
            sums2_ref[r, 2:3, :] = jnp.sum(low.astype(F32), axis=0, keepdims=True)
            return carry

        lax.fori_loop(0, rows, one_row, 0)

    away = pl.ds(pl.multiple_of((1 - core) * half, half), half)
    here = pl.ds(pl.multiple_of(core * half, half), half)

    @pl.when((step >= chunks) & (step < 2 * chunks))
    def _():
        chunk = chunk_of(step, core, chunks)
        cols = pl.ds(pl.multiple_of(chunk * D, D), D)
        total = jnp.zeros((1, D), F32)
        for r in range(rows):
            at = pl.ds(r * length, length)
            grad_act = mm(gdl_ref[at, :], down_ref[...], NT)
            low = (grad_act * slope_ref[at, cols].astype(F32)).astype(BF)
            slope_ref[at, cols] = low
            total += jnp.sum(low.astype(F32), axis=0, keepdims=True)
            acc_ref[at, :] += mm(low, up_ref[...], NT)
        ups_ref[:, cols] = total
        low = slope_ref[:, cols]
        send_up_ref[...] = mm(mid_ref[:, away], low, TN).astype(BF)
        keep_up_ref[...] = mm(mid_ref[:, here], low, TN).astype(BF)

    for first, out in ((chunks, send_down_ref), (chunks + chunks // 2, keep_down_ref)):

        @pl.when((step >= first) & (step < first + chunks // 2))
        def _(out=out):
            cols = pl.ds(pl.multiple_of(chunk_of(step, core, chunks) * D, D), D)
            out[...] = mm(act_ref[:, cols], gdl_ref[...], TN).astype(BF)

    @pl.when(step == 2 * chunks)
    def _():
        def one_row(r, carry):
            at = pl.ds(pl.multiple_of(r * length, length), length)
            grad_mid = acc_ref[at, :]
            normed = xhat_ref[r]
            scaled = grad_mid * g1_ref[...]
            grad_h1 = inv_ref[r, :, 0:1] * (scaled - row_mean(scaled) - normed * row_mean(scaled * normed))
            gh1_ref[r] = grad_h1
            low = grad_h1.astype(BF)
            gal_ref[r] = low
            gdl_ref[at, :] = low
            sums1_ref[r, 0:1, :] = jnp.sum(grad_mid * normed, axis=0, keepdims=True)
            sums1_ref[r, 1:2, :] = jnp.sum(grad_mid, axis=0, keepdims=True)
            sums1_ref[r, 2:3, :] = jnp.sum(low.astype(F32), axis=0, keepdims=True)
            return carry

        lax.fori_loop(0, rows, one_row, 0)
        send_up_ref[...] = mm(ctxt_ref[away, :], gdl_ref[...]).astype(BF)
        keep_up_ref[...] = mm(ctxt_ref[here, :], gdl_ref[...]).astype(BF)


def chunk_of(step, core, chunks):
    back = step - chunks
    half = chunks // 2
    later = back - half
    return jnp.where(step < chunks, step, jnp.where(back < half, (1 - core) * half + back, core * half + jnp.minimum(later, half - 1)))


def run_feed_both(sides, xhat, inv, counts, pooled_grad, ctxt, g1, s1, up, upb, down, downb, g2, s2):
    rows, length, _ = xhat.shape
    tokens, chunks, half = rows * length, FF // D, D // 2
    halves = chunks // 2
    vectors = [g1[None], s1[None], upb[None], downb[None], g2[None], s2[None]]
    ready = [xhat, inv, counts, pooled_grad, from_far(ctxt), *vectors]
    own = lambda *tail: pl.BlockSpec((rows,) + tail, lambda t, sd: (sd[2],) + (0,) * len(tail), pipeline_mode=pl.Buffered(1))
    fixed = lambda shape: pl.BlockSpec(shape, lambda t, sd: (0,) * len(shape), pipeline_mode=pl.Buffered(1))
    backward = lambda t, sd: chunk_of(jnp.maximum(t, chunks), sd[0], chunks)
    up_at = lambda t, sd: (0, jnp.where(t < 2 * chunks, backward(t, sd), chunks))
    return pl.pallas_call(
        feed_both,
        grid_spec=pltpu.PrefetchScalarGridSpec(
            num_scalar_prefetch=1,
            grid=(2 * chunks + 1,),
            in_specs=[fixed(xhat.shape), fixed(inv.shape), own(1, SEGS), own(SEGS, D)]
            + [fixed(v.shape) for v in ready[4:]]
            + [pl.BlockSpec((D, D), lambda t, sd: (0, chunk_of(t, sd[0], chunks))), pl.BlockSpec((D, D), lambda t, sd: (chunk_of(t, sd[0], chunks), 0))],
            out_specs=[
                pl.BlockSpec((D, D), lambda t, sd: (jnp.clip(t - chunks, 0, halves - 1), 0)),
                pl.BlockSpec((D, D), lambda t, sd: (jnp.clip(t - chunks - halves, 0, halves - 1), 0)),
                pl.BlockSpec((half, D), up_at),
                pl.BlockSpec((half, D), up_at),
                fixed((rows, length, D)),
                fixed((rows, length, D)),
                fixed((rows, SEGS, D)),
                fixed((rows, 8, D)),
                fixed((rows, 8, D)),
                fixed((1, FF)),
            ],
            scratch_shapes=[
                pltpu.VMEM((tokens, D), BF),
                pltpu.VMEM((tokens, FF), BF),
                pltpu.VMEM((tokens, FF), BF),
                pltpu.VMEM((tokens, D), BF),
                pltpu.VMEM((tokens, D), F32),
            ],
        ),
        out_shape=[
            far((FF // 2, D), BF),
            far((FF // 2, D), BF),
            far((half, FF + D), BF),
            far((half, FF + D), BF),
            far((rows, length, D), F32),
            jax.ShapeDtypeStruct((rows, length, D), BF),
            jax.ShapeDtypeStruct((rows, SEGS, D), F32),
            jax.ShapeDtypeStruct((rows, 8, D), F32),
            jax.ShapeDtypeStruct((rows, 8, D), F32),
            jax.ShapeDtypeStruct((1, FF), F32),
        ],
        compiler_params=params(46),
        cost_estimate=busy(50),
        name="feed_both",
    )(sides, *ready, from_far(up), from_far(down))


GROUP = 2
GROUP_WIDTH = GROUP * PAIR


def attend_backward(at_ref, gal_ref, q_ref, k_ref, v_ref, lse_ref, cnt_ref, wo_ref, gqkv_ref, sums_ref, mask_ref, gctx_ref):
    length = gal_ref.shape[0]
    gctx_ref[...] = mm(gal_ref[...], wo_ref[...], NT).astype(BF)
    fill_mask(mask_ref, cnt_ref[...])
    low_strip = lax.broadcasted_iota(jnp.int32, (STRIP, PAIR), 1) < HEAD_DIM
    low = lax.broadcasted_iota(jnp.int32, (length, PAIR), 1) < HEAD_DIM

    def pair_step(p, carry):
        at = pl.multiple_of(p * PAIR, PAIR)
        keys = k_ref[:, pl.ds(at, PAIR)]
        values = v_ref[:, pl.ds(at, PAIR)]
        key_of = [jnp.where(low, keys, BF(0)), jnp.where(low, BF(0), keys)]
        grad_k = jnp.zeros((length, PAIR), F32)
        grad_v = jnp.zeros((length, PAIR), F32)
        for s in range(length // STRIP):
            rows = pl.ds(s * STRIP, STRIP)
            lses = lse_ref[pl.ds(pl.multiple_of(8 * p, 8), 8), rows]
            queries = q_ref[rows, pl.ds(at, PAIR)]
            grads = gctx_ref[rows, pl.ds(at, PAIR)]
            grad_q = jnp.zeros((STRIP, PAIR), F32)
            for h in range(2):
                pick = (lambda v: jnp.where(low_strip, v, BF(0))) if h == 0 else (lambda v: jnp.where(low_strip, BF(0), v))
                query, grad = pick(queries), pick(grads)
                scores = mm(keys, query, NT) + mask_ref[:, rows]
                probs = jnp.exp(scores - lses[h : h + 1, :])
                grad_p = mm(values, grad, NT)
                inner = jnp.sum(probs * grad_p, axis=0, keepdims=True)
                grad_s = (probs * (grad_p - inner)).astype(BF)
                grad_v += mm(probs.astype(BF), grad)
                grad_k += mm(grad_s, query)
                grad_q += mm(grad_s, key_of[h], TN)
            gqkv_ref[rows, pl.ds(at, PAIR)] = (grad_q * HEAD_DIM**-0.5).astype(BF)
        gqkv_ref[:, pl.ds(GROUP_WIDTH + at, PAIR)] = grad_k.astype(BF)
        gqkv_ref[:, pl.ds(2 * GROUP_WIDTH + at, PAIR)] = grad_v.astype(BF)
        return carry

    lax.fori_loop(0, GROUP, pair_step, 0)
    sums_ref[...] = jnp.sum(gqkv_ref[...].astype(F32), axis=0, keepdims=True)


def run_attend_backward(group, at, gal, qkv, lse, counts, wo):
    rows, length, _ = gal.shape
    groups = D // GROUP_WIDTH
    row_spec = lambda *tail: pl.BlockSpec((None,) + tail, lambda r, at: (r,) + (0,) * len(tail))
    part = lambda c: pl.BlockSpec((None, length, GROUP_WIDTH), lambda r, at: (r, 0, c * groups + group))
    return pl.pallas_call(
        attend_backward,
        grid_spec=pltpu.PrefetchScalarGridSpec(
            num_scalar_prefetch=1,
            grid=(rows,),
            in_specs=[
                row_spec(length, D), part(0), part(1), part(2),
                pl.BlockSpec((None, 8 * GROUP, length), lambda r, at: (r, group, 0)),
                pl.BlockSpec((None, 1, SEGS), lambda r, at: (at[0] * rows + r, 0, 0)),
                pl.BlockSpec((GROUP_WIDTH, D), lambda r, at: (group, 0)),
            ],
            out_specs=[row_spec(length, 3 * GROUP_WIDTH), row_spec(1, 3 * GROUP_WIDTH)],
            scratch_shapes=[pltpu.VMEM((length, length), F32), pltpu.VMEM((length, GROUP_WIDTH), BF)],
        ),
        out_shape=[jax.ShapeDtypeStruct((rows, length, 3 * GROUP_WIDTH), BF), jax.ShapeDtypeStruct((rows, 1, 3 * GROUP_WIDTH), F32)],
        compiler_params=params(20),
        cost_estimate=busy(14),
        name="attend_backward",
    )(at, gal, qkv, qkv, qkv, lse, counts, from_far(wo))


def input_grad(at_ref, gh1_ref, *refs):
    parts, (wqkv_ref, own_ref, send_ref) = refs[:-3], refs[-3:]
    half = gh1_ref.shape[0] // 2
    for out, first in ((own_ref, at_ref[0]), (send_ref, 1 - at_ref[0])):
        rows = pl.ds(pl.multiple_of(first * half, half), half)
        total = gh1_ref[rows, :]
        for g, part in enumerate(parts):
            for c in range(3):
                total += mm(part[rows, c * GROUP_WIDTH : (c + 1) * GROUP_WIDTH], wqkv_ref[:, c * D + g * GROUP_WIDTH : c * D + (g + 1) * GROUP_WIDTH], NT)
        out[...] = total.astype(BF)


def run_input_grad(at, gh1, parts, wqkv):
    rows, length, _ = gh1.shape
    half = length // 2
    row_spec = lambda *tail: pl.BlockSpec((None,) + tail, lambda r, at: (r,) + (0,) * len(tail))
    return pl.pallas_call(
        input_grad,
        grid_spec=pltpu.PrefetchScalarGridSpec(
            num_scalar_prefetch=1,
            grid=(rows,),
            in_specs=[row_spec(length, D)] + [row_spec(length, 3 * GROUP_WIDTH)] * len(parts) + [whole((D, 3 * D))],
            out_specs=[row_spec(half, D), row_spec(half, D)],
        ),
        out_shape=[jax.ShapeDtypeStruct((rows, half, D), BF)] * 2,
        compiler_params=params(18),
        cost_estimate=busy(6),
        name="input_grad",
    )(at, from_far(gh1), *parts, from_far(wqkv))


SMALLS = 128


def gather_small(sums1_ref, sums2_ref, ups_ref, sq_refs, small_ref, pack_ref):
    pack_ref[...] = jnp.zeros_like(pack_ref)
    total = lambda ref: jnp.sum(ref[...], axis=0)
    first, second, ups = total(sums1_ref), total(sums2_ref), ups_ref[...]
    for g, ref in enumerate(sq_refs):
        cols = slice(g * GROUP_WIDTH, (g + 1) * GROUP_WIDTH)
        pack_ref[0:1, cols] = total(ref)[:, :GROUP_WIDTH]
        pack_ref[1:2, cols] = total(ref)[:, 2 * GROUP_WIDTH :]
    lines = [first[2:3], first[0:1], first[1:2], second[2:3], second[0:1], second[1:2]]
    lines += [ups[:, i * D : (i + 1) * D] for i in range(FF // D)]
    for i, line in enumerate(lines):
        pack_ref[i + 2 : i + 3, :] = line
    small_ref[...] = jnp.transpose(pack_ref[...])


def qkv_grads_body(parts, sides_ref, x_away_ref, x_here_ref, *refs):
    grads, refs = refs[:parts], refs[parts:]
    small_in, (away_ref, here_ref, small_ref, pack_ref) = refs[:-4], refs[-4:]
    half, wide = x_away_ref.shape[0], 3 * GROUP_WIDTH
    gather_small(*small_in[:3], small_in[3:], small_ref, pack_ref)
    for left, out, first in ((x_away_ref, away_ref, 1 - sides_ref[0]), (x_here_ref, here_ref, sides_ref[0])):
        for g, grad in enumerate(grads):
            out[:, g * wide : (g + 1) * wide] = mm(left[...], grad[...]).astype(BF)
        rows = pl.ds(pl.multiple_of(first * half, half), half)
        out[:, parts * wide :] = small_ref[rows, :].astype(BF)


def qkv_grads(sides, x, grads, smalls):
    half, tokens = D // 2, x.shape[1]
    width = 3 * GROUP_WIDTH * len(grads) + SMALLS
    return pl.pallas_call(
        functools.partial(qkv_grads_body, len(grads)),
        grid_spec=pltpu.PrefetchScalarGridSpec(
            num_scalar_prefetch=1,
            grid=(1,),
            in_specs=[pl.BlockSpec((half, tokens), lambda j, sd: (1 - sd[0], 0)), pl.BlockSpec((half, tokens), lambda j, sd: (sd[0], 0))]
            + [whole(v.shape) for v in (*grads, *smalls)],
            out_specs=[pl.BlockSpec((half, width), lambda j, sd: (0, 0))] * 2,
            scratch_shapes=[pltpu.VMEM((D, SMALLS), F32), pltpu.VMEM((SMALLS, D), F32)],
        ),
        out_shape=[far((half, width), BF)] * 2,
        compiler_params=params(24),
        cost_estimate=busy(7),
        name="qkv_grads",
    )(sides, *[from_far(x)] * 2, *grads, *smalls)


def add_split_body(at_ref, keep_away_ref, keep_here_ref, got_away_ref, got_here_ref, send_ref, next_ref):
    send_ref[...] = (keep_away_ref[...].astype(F32) + got_away_ref[...].astype(F32)).astype(BF)
    next_ref[...] = (keep_here_ref[...].astype(F32) + got_here_ref[...].astype(F32)).astype(BF)


def add_split(at, keep, got):
    half, width = keep.shape[0] // 2, keep.shape[1]
    cols = width // 2 if width % 256 == 0 else width
    away = pl.BlockSpec((half, cols), lambda j, at: (1 - at[0], j))
    here = pl.BlockSpec((half, cols), lambda j, at: (at[0], j))
    return pl.pallas_call(
        add_split_body,
        grid_spec=pltpu.PrefetchScalarGridSpec(
            num_scalar_prefetch=1,
            grid=(width // cols,),
            in_specs=[away, here, away, here],
            out_specs=[pl.BlockSpec((half, cols), lambda j, at: (0, j))] * 2,
        ),
        out_shape=[far((half, width), BF), far((half, width), BF)],
        compiler_params=params(16),
        cost_estimate=busy(3),
        name="add_split",
    )(at, *[from_far(keep)] * 2, got, got)


def assemble_body(steps, moves, place_ref, *refs):
    outs = refs[len(refs) - len(moves) :]
    pieces = refs[: len(refs) - len(moves)]
    at = pl.program_id(0) // steps
    for p in range(4):

        @pl.when(at == p)
        def _(p=p):
            for out, parts in zip(outs, moves):
                for source, first, width, to in parts:
                    out[:, to : to + width] = pieces[4 * source + p][:, first : first + width].astype(F32)


def assemble(places, sources, moves):
    quarter = sources[0][0].shape[0]
    block = min(quarter, 384)
    steps = quarter // block
    widths = [sum(part[2] for part in parts) for parts in moves]
    piece_at = lambda p, width: pl.BlockSpec((block, width), lambda i, pos: (jnp.clip(i - p * steps, 0, steps - 1), 0))
    return pl.pallas_call(
        functools.partial(assemble_body, steps, moves),
        grid_spec=pltpu.PrefetchScalarGridSpec(
            num_scalar_prefetch=1,
            grid=(4 * steps,),
            in_specs=[piece_at(p, pieces[p].shape[1]) for pieces in sources for p in range(4)],
            out_specs=[pl.BlockSpec((block, w), lambda i, pos: (pos[i // steps] * steps + i % steps, 0)) for w in widths],
        ),
        out_shape=[jax.ShapeDtypeStruct((4 * quarter, w), F32) for w in widths],
        compiler_params=params(36),
        cost_estimate=busy(8),
        name="assemble",
    )(places, *[piece for pieces in sources for piece in pieces])


class Links:
    def __init__(self):
        dp, seq = lax.axis_size("dp"), lax.axis_size("seq")
        dp_at, seq_at = lax.axis_index("dp"), lax.axis_index("seq")
        self.core = dp_at % 2

        def flip(bit_of):
            pairs = []
            for d in range(dp):
                for s in range(seq):
                    bit = bit_of(d % 2)
                    to = (d, s ^ 1) if bit < 0 else (d ^ (1 << bit), s)
                    pairs.append((d * seq + s, to[0] * seq + to[1]))
            return pairs

        second = (dp_at >> 1) % 2
        self.side_a = jnp.where(self.core == 0, second, seq_at)
        self.side_b = jnp.where(self.core == 0, seq_at, second)
        self.pairs_core = flip(lambda c: 0)
        self.pairs_a = flip(lambda c: 1 if c == 0 else -1)
        self.pairs_b = flip(lambda c: -1 if c == 0 else 1)
        bits = list(range(2, (dp - 1).bit_length()))
        self.rest = []
        for first in range(0, len(bits)):
            part = bits[first : first + 1]
            size = 1 << len(part)
            routes = [[(d * seq + s, (d ^ (hop << part[0])) * seq + s) for d in range(dp) for s in range(seq)] for hop in range(1, size)]
            self.rest.append((routes, (dp_at >> part[0]) % size))
        self.sides = jnp.stack([self.core, self.side_a, seq_at]).astype(jnp.int32)
        self.side_a_array = self.side_a.astype(jnp.int32).reshape(1)
        self.side_b_array = self.side_b.astype(jnp.int32).reshape(1)
        other = 2 * (1 - self.core)
        mine = 2 * self.core
        self.places = jnp.stack([mine + self.side_a, mine + 1 - self.side_a, other + self.side_b, other + 1 - self.side_b]).astype(jnp.int32)

    def send(self, value, pairs):
        return lax.ppermute(value, ("dp", "seq"), pairs)


class Order:
    def __init__(self):
        self.last = None

    def run(self, step, first, *others):
        if self.last is not None:
            first, self.last = lax.optimization_barrier((first, self.last))
        out = step(first, *others)
        self.last = jax.tree.leaves(out)[0]
        return out

    def arrive(self, value):
        value, self.last = lax.optimization_barrier((value, self.last))
        return value


def collect(at, pieces):
    swap = 1
    while swap < len(pieces):
        bit = (at // swap) % 2
        pieces = [jnp.where(bit == 0, pieces[i], pieces[i ^ swap]) for i in range(len(pieces))]
        swap *= 2
    return jnp.concatenate(pieces)


def exchange(order, links, away, keep, done, finish):
    got = links.send(away, links.pairs_core)
    yield
    away, keep = order.run(lambda g: add_split(links.side_a_array, keep, g), got)
    got = links.send(away, links.pairs_a)
    yield
    away, keep = order.run(lambda g: add_split(links.side_b_array, keep, g), got)
    got = links.send(away, links.pairs_b)
    yield
    for routes, at in links.rest:
        piece = keep.shape[0] // (len(routes) + 1)

        def deal(got, keep=keep, at=at, piece=piece, routes=routes):
            part = lambda v, to: lax.dynamic_slice_in_dim(v, to * piece, piece, 0).astype(F32)
            both = lambda to: part(keep, to) + part(got, to)
            return [both(at ^ hop).astype(BF) for hop in range(1, len(routes) + 1)], both(at)

        parts, keep = order.run(deal, got)
        got = [links.send(p, pairs) for p, pairs in zip(parts, routes)]
        yield
        got = order.run(lambda g, *rest: sum(v.astype(F32) for v in (g, *rest)), *got)
    cur = (keep.astype(F32) + got.astype(F32)).astype(BF)
    for routes, at in links.rest[::-1]:
        got = [links.send(cur, pairs) for pairs in routes]
        yield
        cur = order.run(lambda g, *rest: collect(at, [cur, g, *rest]), *got)
    got = links.send(cur, links.pairs_b)
    yield
    cur = order.run(lambda g: collect(links.side_b, [cur, g]), got)
    got = links.send(cur, links.pairs_a)
    across = links.send(cur, links.pairs_core)
    yield
    got = order.arrive(got)
    done.append([cur, got, across, links.send(got, links.pairs_core)])
    yield
    if finish is not None:
        done.append(order.run(lambda g: finish([cur, got, across, g]), done[0][3]))
        yield


SCHEDULE = "mdummdmdudqudmuqdududmqmuqqudqddququuqqu"


def swap_seq(value):
    return lax.ppermute(value, "seq", [(0, 1), (1, 0)])


def local(
    hidden_in,
    segment_ids,
    segment_counts,
    pooled_grad,
    qkv_weight,
    query_bias,
    value_bias,
    out_weight,
    out_bias,
    norm1_gain,
    norm1_shift,
    up_weight,
    up_bias,
    down_weight,
    down_bias,
    norm2_gain,
    norm2_shift,
):
    links = Links()
    seq_at = lax.axis_index("seq")
    seq_array = seq_at.astype(jnp.int32).reshape(1)
    micro, row_count, piece, _ = hidden_in.shape
    length = piece * 2
    own_micro = micro // 2
    rows = own_micro * row_count
    tokens = rows * length

    hidden = hidden_in.reshape(micro * row_count, piece, D)
    got = []
    for row in range(rows):
        away = lax.dynamic_index_in_dim(hidden, (1 - seq_at) * rows + row, 0, keepdims=False)
        if got:
            away = lax.optimization_barrier((away, got[-1]))[0]
        got.append(swap_seq(away))
    counts = segment_counts.reshape(micro * row_count, 1, SEGS)
    pooled_cot = pooled_grad.reshape(micro * row_count, SEGS, D)
    order = Order()
    seen = []
    for row in range(rows):
        seen = run_attend_forward(row, rows, seq_array, hidden, got[row], counts, qkv_weight, query_bias, value_bias, out_weight, out_bias, seen)
    qkv, x_turned, ctx_turned, lse, xhat, inv = seen
    order.last = xhat
    away_down, keep_down, away_up, keep_up, grad_h1, grad_attn_low, pooled, sums1, sums2, ups = run_feed_both(
        links.sides, xhat, inv, counts, pooled_cot, ctx_turned, norm1_gain, norm1_shift,
        up_weight, up_bias, down_weight, down_bias, norm2_gain, norm2_shift,
    )
    order.last = away_down
    streams, sums, state = {}, {name: [] for name in ("down", "up", "qkv")}, {}
    finishes = {
        "down": lambda pieces: assemble(links.places, [pieces], [[(0, 0, D, 0)]]),
        "up": lambda pieces: assemble(links.places, [pieces], [[(0, 0, FF, 0)], [(0, FF, D, 0)]]),
    }

    def start(name, away, keep):
        streams[name] = exchange(order, links, away, keep, sums[name], finishes.get(name))
        next(streams[name])

    def joined(first, second):
        return jnp.where(seq_at == 0, jnp.concatenate([first, second]), jnp.concatenate([second, first]))

    def main_steps():
        start("down", away_down, keep_down)
        start("up", away_up, keep_up)
        pooled_own = pooled.reshape(own_micro, row_count, SEGS, D)
        pooled_got = swap_seq(pooled_own)
        grads, sums_qkv = [], []
        for group in range(D // GROUP_WIDTH):
            grad, total = order.run(lambda g: run_attend_backward(group, seq_array, g, qkv, lse, counts, out_weight), grad_attn_low)
            grads.append(grad)
            sums_qkv.append(total)
            yield
        flat = [g.reshape(tokens, 3 * GROUP_WIDTH) for g in grads]
        smalls = (sums1, sums2, ups, *sums_qkv)
        start("qkv", *order.run(lambda g: qkv_grads(links.sides, x_turned, [*flat[:-1], g], smalls), flat[-1]))
        yield
        back_own, back_send = order.run(lambda g: run_input_grad(seq_array, g, grads, qkv_weight), grad_h1)
        shape = (own_micro, row_count, piece, D)
        back_own, back_got = back_own.reshape(shape), swap_seq(back_send.reshape(shape))
        yield
        state["pooled"] = order.run(lambda g: joined(pooled_own, g), pooled_got)
        yield
        state["input"] = order.run(lambda g: joined(back_own, g), back_got)
        yield

    streams["main"] = main_steps()
    for name in map({"m": "main", "d": "down", "u": "up", "q": "qkv"}.get, SCHEDULE):
        if name in streams:
            next(streams[name], None)
    while streams:
        for name in list(streams):
            if next(streams[name], streams) is streams:
                del streams[name]
    pooled_local, input_local = state["pooled"], state["input"]
    (down_all,) = sums["down"][1]
    up_all, out_all = sums["up"][1]
    wide = 3 * GROUP_WIDTH
    columns = [(0, g * wide + c * GROUP_WIDTH, GROUP_WIDTH, c * D + g * GROUP_WIDTH) for g in range(D // GROUP_WIDTH) for c in range(3)]
    qkv_all, small_all = assemble(links.places, sums["qkv"], [columns, [(0, 3 * D, SMALLS, 0)]])
    lines = small_all[:, : 8 + FF // D].T
    return (
        pooled_local,
        input_local,
        qkv_all,
        lines[0],
        lines[1],
        out_all,
        lines[2],
        lines[3],
        lines[4],
        up_all,
        lines[8 : 8 + FF // D].reshape(FF),
        down_all,
        lines[5],
        lines[6],
        lines[7],
    )


def solution(mesh):
    rep = P()
    in_specs = (
        P(None, "dp", "seq", None),
        P(None, "dp", "seq"),
        P(None, "dp", None),
        P(None, "dp", None, None),
    ) + (rep,) * 13
    out_specs = (P(None, "dp", None, None), P(None, "dp", "seq", None)) + (rep,) * 13
    return jax.shard_map(local, mesh=mesh, in_specs=in_specs, out_specs=out_specs, check_vma=False)
```
